256 devices in a mesh: seq: 64 (over y, z, core), tp: 4 (over x).
Axes of the slice: x: 4, y: 4, z: 8, core: 2. Of those that a mesh axis runs over, the one named last changes fastest.
Arguments:
- stream: bfloat16 [8192, 2048], P('seq'), may hold values from -256 to 256
- lengths: int32 [6], replicated, may hold values from 1 to 7168, 8192 in all
- q_weight: bfloat16 [2048, 1536], P(None, 'tp'), may hold values from -0.125 to 0.125
- kv_down: bfloat16 [2048, 576], replicated, may hold values from -0.125 to 0.125
- latent_gain: float32 [512], replicated, may hold values from 0.1 to 1.9
- kv_up: bfloat16 [8, 512, 256], P('tp'), may hold values from -0.25 to 0.25
- out_weight: bfloat16 [1024, 2048], P('tp'), may hold values from -0.1875 to 0.1875
- moe_gain: float32 [2048], replicated, may hold values from 0.1 to 1.9
- routes: int32 [8192, 6], P('seq'), may hold values from 0 to 63, all different within a row; in each aligned block of 128 rows (0 to 127, 128 to 255, ...) at most 24 rows name the same one
- route_weight: float32 [8192, 6], P('seq'), may hold values from 0.05 to 0.5
- expert_gate: bfloat16 [64, 2048, 1408], P('seq', None, 'tp'), may hold values from -0.125 to 0.125
- expert_up: bfloat16 [64, 2048, 1408], P('seq', None, 'tp'), may hold values from -0.125 to 0.125
- expert_down: bfloat16 [64, 1408, 2048], P('seq', 'tp'), may hold values from -0.15625 to 0.15625
Outputs:
- layer_out: bfloat16 [8192, 2048], P('seq')
- latent_cache: bfloat16 [8192, 576], P('seq')
The draws below stay inside these ranges and needn't reach their ends.
Inputs may be any that keep to these rules, and one draw needn't show every extreme that they name: 6 lengths summing to 8192, the longest exactly 7168. In each aligned block of 128 rows no expert is named by more than 24 routes, a bound that some block reaches.
All inputs are finite; a program needn't handle non-finite values.
Results may differ from the reference program's by a relative error of at most 0.0075.
Values may be sent and summed in bfloat16 or wider, within the bound.
A program may use at most 128 MiB of HBM per device.

```python
import math
import jax
import jax.numpy as jnp
import numpy as np
from jax import lax

D = 2048
HEADS = 8
NOPE = 128
ROPE = 64
LATENT = 512
VDIM = 128
FF = 1408
TOP = 6
SEGS = 6
TOK_DEV = 128
TOKENS = 8192
LONGEST = 7168
EXPERTS = 64
CAP = 24
N_SEQ = 64
N_TP = 4


def draw_stream(key, part):
    values_raw = jnp.clip(jax.random.normal(key, (TOKENS, D), jnp.float32), -5.0, 5.0)
    return values_raw.astype(jnp.bfloat16)


def block_scale(rng, shape, shards, low, top_value):
    loudness, own = 1.0, jax.random.fold_in(rng, 6)
    for dim, parts in shards:
        draws = jnp.exp(jax.random.uniform(jax.random.fold_in(own, dim), (parts,), jnp.float32, low / len(shards), top_value / len(shards)))
        loudness = loudness * jnp.repeat(draws, shape[dim] // parts).reshape([-1 if axis == dim else 1 for axis in range(len(shape))])
    return loudness


def profile(number_of, total, reach, lean):
    loads = [(1 << 20) // math.isqrt(standing ** lean) + 1 for standing in range(2, number_of + 1)]
    rest, holding = total - reach - (number_of - 1), [1] * (number_of - 1)
    while rest > 0:
        free = [i for i in range(number_of - 1) if holding[i] < reach]
        mass, left = sum([loads[i] for i in free]), rest
        for i in free:
            addition = min(reach - holding[i], max(1, left * loads[i] // mass), rest)
            holding[i] = holding[i] + addition
            rest = rest - addition
    return np.array([reach] + holding)


def ragged(own_key, number_of, total, most, slope):
    if number_of == 2:
        one = jax.random.randint(own_key, (), max(1, total - most), min(most, total - 1) + 1)
        return jnp.stack([one, total - one])
    tallies = jnp.asarray(profile(number_of, total, most, slope), jnp.int32)
    couples = (number_of - 1) // 2
    donor, sink = tallies[1:1 + 2 * couples:2], tallies[2:2 + 2 * couples:2]
    margin = jnp.minimum(donor - 1, most - sink)
    moved = jax.random.randint(jax.random.fold_in(own_key, 1), (couples,), 0, 1 << 20) % (margin + 1)
    tallies = tallies.at[1:1 + 2 * couples:2].set(donor - moved).at[2:2 + 2 * couples:2].set(sink + moved)
    return tallies[jax.random.permutation(jax.random.fold_in(own_key, 2), number_of)]


def assign_block(stream_key, own, number, rows, count, top, most, lean):
    sequence = jax.random.permutation(stream_key, count)
    packed, usual = load_shares(count, rows * top, most, lean, True), load_shares(count, rows * top, most, lean, False)
    places = jnp.arange(count)

    def named(sizes, offset_by):
        used = int((sizes > 0).sum())
        fixed = max(1, used // 4)
        moved = fixed + (places - fixed + offset_by * (used - fixed)) % max(1, count - fixed)
        return jnp.zeros((count,), jnp.int32).at[sequence[jnp.where(places < fixed, places, moved)]].set(jnp.asarray(sizes, jnp.int32))

    sizes = jnp.where(number % 4 == 0, named(packed, number // 4), named(usual, number - number // 4 - 1))
    mixed = jax.random.permutation(jax.random.fold_in(own, 3), count)
    donor, sink = mixed[0:count // 2 * 2:2], mixed[1:count // 2 * 2:2]
    margin = jnp.minimum(sizes[donor] - 1, most - sizes[sink]) // 2
    margin = jnp.where((donor == sequence[0]) | (sink == sequence[0]) | (sizes[sink] == 0), 0, jnp.maximum(margin, 0))
    moved = jax.random.randint(jax.random.fold_in(own, 4), (count // 2,), 0, 1 << 20) % (margin + 1)
    sizes = sizes.at[donor].add(-moved).at[sink].add(moved)
    labels = jnp.searchsorted(jnp.cumsum(sizes), jnp.arange(rows * top), side="right").astype(jnp.int32)
    table = labels.reshape(top, rows).T
    table = table[jax.random.permutation(jax.random.fold_in(own, 1), rows)]
    offset_by = jax.random.randint(jax.random.fold_in(own, 2), (rows, 1), 0, top)
    return jnp.take_along_axis(table, (jnp.arange(top)[None, :] + offset_by) % top, axis=1)


def load_shares(count, total, bound, skew, full):
    portions = [(1 << 20) // math.isqrt(rank ** skew) + 1 for rank in range(1, count + 1)]
    largest = bound if full else min(bound, max(-(-total // count), total * portions[0] // sum(portions)))
    least = 1 if total - largest >= count - 1 else 0
    given, spare = [largest] + [least] * (count - 1), total - largest - least * (count - 1)
    while spare > 0:
        movable = [i for i in range(1, count) if given[i] < largest] or [i for i in range(1, count) if given[i] < bound]
        whole, left = sum([portions[i] for i in movable]), spare
        for i in movable:
            more = min(bound - given[i], max(1, left * portions[i] // whole), spare)
            given[i] = given[i] + more
            spare = spare - more
    return np.array(given)


def bell_draw(rng, extent, spread, limit, cuts=(), kind=jnp.bfloat16):
    entries = jax.random.normal(rng, extent, jnp.float32) * spread
    if len(cuts) > 0:
        entries = block_scale(rng, extent, cuts, -0.22, 0.18) * entries
    return jnp.clip(entries, min=-limit, max=limit).astype(kind)


def setup_inputs(seed: int = 0) -> dict:
    streams_of = jax.random.split(jax.random.key(seed), 14)
    stream = draw_stream(jax.random.fold_in(streams_of[13], 71), 0)
    lengths = ragged(streams_of[1], SEGS, TOKENS, LONGEST, 2).astype(jnp.int32)
    q_weight = bell_draw(streams_of[2], (D, HEADS * (NOPE + ROPE)), D ** -0.5, 0.125, ((1, 4),))
    kv_down = bell_draw(streams_of[3], (D, LATENT + ROPE), D ** -0.5, 0.125)
    latent_gain = jnp.clip(1.0 + 0.18 * jax.random.normal(streams_of[4], (LATENT,), jnp.float32), 0.1, 1.9)
    kv_up = bell_draw(streams_of[5], (HEADS, LATENT, NOPE + VDIM), LATENT ** -0.5, 0.25, ((0, 4),))
    out_weight = bell_draw(streams_of[6], (HEADS * VDIM, D), (HEADS * VDIM) ** -0.5, 0.1875, ((0, 4),))
    moe_gain = jnp.clip(1.0 + 0.18 * jax.random.normal(streams_of[7], (D,), jnp.float32), 0.1, 1.9)
    routes_keys = jax.random.split(jax.random.fold_in(streams_of[8], 1), TOKENS // TOK_DEV)
    routes_turns = jax.random.permutation(jax.random.fold_in(streams_of[8], 3), TOKENS // TOK_DEV)
    routes = jax.vmap(lambda own, number: assign_block(jax.random.fold_in(streams_of[8], 2), own, number, TOK_DEV, EXPERTS, TOP, CAP, 2))(routes_keys, routes_turns).reshape((TOKENS, TOP))
    route_weight = jnp.clip(jnp.exp(math.log(0.5) - 2.3025851 * jax.random.uniform(streams_of[9], (TOKENS, TOP), jnp.float32) ** block_scale(streams_of[9], (TOKENS, TOP), ((0, 64),), -0.2, 0.2)), 0.05, 0.5)
    expert_gate = bell_draw(streams_of[10], (EXPERTS, D, FF), D ** -0.5, 0.125, ((0, 64), (2, 4)))
    expert_up = bell_draw(streams_of[11], (EXPERTS, D, FF), D ** -0.5, 0.125, ((0, 64), (2, 4)))
    expert_down = bell_draw(streams_of[12], (EXPERTS, FF, D), FF ** -0.5, 0.15625, ((0, 64), (1, 4)))
    return {"stream": stream, "lengths": lengths, "q_weight": q_weight, "kv_down": kv_down, "latent_gain": latent_gain, "kv_up": kv_up, "out_weight": out_weight, "moe_gain": moe_gain, "routes": routes, "route_weight": route_weight, "expert_gate": expert_gate, "expert_up": expert_up, "expert_down": expert_down}


THETA = 50000.0

def place(token_index, lengths):
    prompt_ends = jnp.cumsum(lengths)
    before = (prompt_ends[None, :] <= token_index[:, None]).astype(jnp.int32)
    segment = lax.optimization_barrier(jnp.sum(before, axis=1))
    prompt_start = lax.optimization_barrier(jnp.sum(before * lengths[None, :], axis=1))
    return (segment, token_index - prompt_start)

def angles(position):
    half_rope = ROPE // 2
    frequency = THETA ** (-2.0 * jnp.arange(half_rope, dtype=jnp.float32) / ROPE)
    angle_table = position.astype(jnp.float32)[:, None] * frequency[None, :]
    return (jnp.cos(angle_table), jnp.sin(angle_table))

def rotate(values, cos_table, sin_table):
    half_rope = ROPE // 2
    first_half = values[..., :half_rope]
    second = values[..., half_rope:]
    return jnp.concatenate([first_half * cos_table - second * sin_table, first_half * sin_table + second * cos_table], axis=-1)

def latent_rows(stream, kv_down, latent_gain, cos_table, sin_table):
    kv_proj = jnp.dot(stream, kv_down, preferred_element_type=jnp.float32)
    compressed = kv_proj[:, :LATENT]
    factor = lax.rsqrt(lax.optimization_barrier(jnp.mean(compressed * compressed, axis=1, keepdims=True)) + 1e-06)
    normed = compressed * factor * latent_gain[None, :]
    return jnp.concatenate([normed, rotate(kv_proj[:, LATENT:], cos_table, sin_table)], axis=1).astype(jnp.bfloat16)

def reference(stream, lengths, q_weight, kv_down, latent_gain, kv_up, out_weight, moe_gain, routes, route_weight, expert_gate, expert_up, expert_down):
    token_index = jnp.arange(TOKENS, dtype=jnp.int32)
    segment, position = place(token_index, lengths)
    cos_table, sin_table = angles(position)
    latent = latent_rows(stream, kv_down, latent_gain, cos_table, sin_table)
    q_proj = jnp.dot(stream, q_weight, preferred_element_type=jnp.float32).astype(jnp.bfloat16)
    q_proj = q_proj.reshape(TOKENS, HEADS, NOPE + ROPE)
    absorbed = jnp.einsum('thj,hcj->thc', q_proj[:, :, :NOPE].astype(jnp.float32), kv_up[:, :, :NOPE].astype(jnp.float32), precision=lax.Precision.HIGHEST)
    rotated = rotate(q_proj[:, :, NOPE:].astype(jnp.float32), cos_table[:, None, :], sin_table[:, None, :])
    softmax_scale = (NOPE + ROPE) ** (-0.5)
    queries = (jnp.concatenate([absorbed, rotated], axis=2) * softmax_scale).astype(jnp.bfloat16)
    keys_f32 = latent.astype(jnp.float32)
    block_rows = min(512, TOKENS)

    def one_block(offset):
        query_block = lax.dynamic_slice_in_dim(queries, offset, block_rows, 0).astype(jnp.float32)
        block_seg = lax.dynamic_slice_in_dim(segment, offset, block_rows, 0)
        block_idx = lax.dynamic_slice_in_dim(token_index, offset, block_rows, 0)
        scores = jnp.einsum('tha,ka->thk', query_block, keys_f32, precision=lax.Precision.HIGHEST)
        allowed = (block_seg[:, None] == segment[None, :]) & (token_index[None, :] <= block_idx[:, None])
        scores = jnp.where(allowed[:, None, :], scores, -jnp.inf)
        block_peak = lax.optimization_barrier(jnp.max(scores, axis=2, keepdims=True))
        weights = jnp.exp(scores - block_peak)
        weight_sum = lax.optimization_barrier(jnp.sum(weights, axis=2))
        probs = lax.optimization_barrier(weights.astype(jnp.bfloat16)).astype(jnp.float32)
        context = jnp.einsum('thk,kc->thc', probs, keys_f32[:, :LATENT], precision=lax.Precision.HIGHEST)
        return context / weight_sum[:, :, None]
    starts = jnp.arange(0, TOKENS, block_rows, dtype=jnp.int32)
    context = lax.map(one_block, starts).reshape(TOKENS, HEADS, LATENT)
    heads_out = jnp.einsum('thc,hcv->thv', context, kv_up[:, :, NOPE:].astype(jnp.float32), precision=lax.Precision.HIGHEST)
    heads_out = heads_out.astype(jnp.bfloat16).reshape(TOKENS, HEADS * VDIM)
    attention = jnp.dot(heads_out, out_weight, preferred_element_type=jnp.float32)
    hidden = stream.astype(jnp.float32) + attention
    normed = (hidden * lax.rsqrt(lax.optimization_barrier(jnp.mean(hidden * hidden, axis=1, keepdims=True)) + 1e-06) * moe_gain[None, :]).astype(jnp.bfloat16)
    most_rows = N_SEQ * CAP
    flat_routes = routes.reshape(-1).astype(jnp.int32)
    route_order = jnp.argsort(flat_routes, stable=True).astype(jnp.int32)
    sorted_routes = flat_routes[route_order]
    expert_ids = jnp.arange(EXPERTS, dtype=jnp.int32)
    starts_e = jnp.searchsorted(sorted_routes, expert_ids, side='left').astype(jnp.int32)
    counts = lax.optimization_barrier(jnp.sum((flat_routes[None, :] == expert_ids[:, None]).astype(jnp.int32), axis=1))
    padded = jnp.concatenate([route_order, jnp.zeros((most_rows,), jnp.int32)])
    flat_weight = route_weight.reshape(-1)
    group_width = FF // N_TP

    def one_expert(moe_total, expert):
        picked_rows = lax.dynamic_slice_in_dim(padded, starts_e[expert], most_rows, 0)
        is_valid = jnp.arange(most_rows, dtype=jnp.int32) < counts[expert]
        token_rows = picked_rows // TOP
        inputs = normed[token_rows]
        gate_act = jnp.dot(inputs, expert_gate[expert], preferred_element_type=jnp.float32)
        up_act = jnp.dot(inputs, expert_up[expert], preferred_element_type=jnp.float32)
        hidden_units = (jax.nn.silu(gate_act) * up_act).astype(jnp.bfloat16)
        down = expert_down[expert]
        expert_out = jnp.zeros((most_rows, D), jnp.float32)
        for group_index in range(N_TP):
            piece_out = jnp.dot(hidden_units[:, group_index * group_width:(group_index + 1) * group_width], down[group_index * group_width:(group_index + 1) * group_width], preferred_element_type=jnp.float32)
            expert_out = expert_out + lax.optimization_barrier(piece_out.astype(jnp.bfloat16)).astype(jnp.float32)
        weight = jnp.where(is_valid, flat_weight[picked_rows], jnp.zeros((), jnp.float32))
        moe_total = moe_total.at[token_rows].add(expert_out * weight[:, None])
        return (moe_total, None)
    moe, unused = lax.scan(one_expert, jnp.zeros((TOKENS, D), jnp.float32), expert_ids)
    layer_out = (hidden + moe).astype(jnp.bfloat16)
    return (layer_out, latent)
```

```python
import jax
import jax.numpy as jnp
from jax import lax
from jax.sharding import PartitionSpec as P

D = 2048
NOPE = 128
ROPE = 64
LATENT = 512
VDIM = 128


THETA = 50000.0


def place(token_index, lengths):
    prompt_ends = jnp.cumsum(lengths)
    before = (prompt_ends[None, :] <= token_index[:, None]).astype(jnp.int32)
    segment = jnp.sum(before, axis=1)
    prompt_start = jnp.sum(before * lengths[None, :], axis=1)
    return (segment, token_index - prompt_start)


def angles(position):
    half_rope = ROPE // 2
    frequency = THETA ** (-2.0 * jnp.arange(half_rope, dtype=jnp.float32) / ROPE)
    angle_table = position.astype(jnp.float32)[:, None] * frequency[None, :]
    return (jnp.cos(angle_table), jnp.sin(angle_table))


def rotate(values, cos_table, sin_table):
    half_rope = ROPE // 2
    first_half = values[..., :half_rope]
    second = values[..., half_rope:]
    return jnp.concatenate(
        [first_half * cos_table - second * sin_table, first_half * sin_table + second * cos_table],
        axis=-1,
    )


def on_device(
    stream,
    lengths,
    q_weight,
    kv_down,
    latent_gain,
    kv_up,
    out_weight,
    moe_gain,
    routes,
    route_weight,
    expert_gate,
    expert_up,
    expert_down,
):
    tok_count = stream.shape[0]
    head_count = kv_up.shape[0]
    first_row = lax.axis_index("seq") * tok_count
    token_index = first_row + jnp.arange(tok_count, dtype=jnp.int32)
    segment, position = place(token_index, lengths)
    cos_table, sin_table = angles(position)
    kv_proj = jnp.dot(stream, kv_down, preferred_element_type=jnp.float32)
    compressed = kv_proj[:, :LATENT]
    factor = lax.rsqrt(jnp.mean(compressed * compressed, axis=1, keepdims=True) + 1e-06)
    latent = jnp.concatenate(
        [
            compressed * factor * latent_gain[None, :],
            rotate(kv_proj[:, LATENT:], cos_table, sin_table),
        ],
        axis=1,
    ).astype(jnp.bfloat16)
    q_proj = jnp.dot(stream, q_weight, preferred_element_type=jnp.float32).astype(jnp.bfloat16)
    q_proj = q_proj.reshape(tok_count, head_count, NOPE + ROPE)
    absorbed = jnp.einsum(
        "thj,hcj->thc", q_proj[:, :, :NOPE], kv_up[:, :, :NOPE], preferred_element_type=jnp.float32
    )
    rotated = rotate(
        q_proj[:, :, NOPE:].astype(jnp.float32), cos_table[:, None, :], sin_table[:, None, :]
    )
    softmax_scale = (NOPE + ROPE) ** (-0.5)
    queries = (jnp.concatenate([absorbed, rotated], axis=2) * softmax_scale).astype(jnp.bfloat16)
    queries = queries.reshape(tok_count * head_count, LATENT + ROPE)
    row_segment = jnp.repeat(segment, head_count)
    row_index = jnp.repeat(token_index, head_count)
    row_total = tok_count * head_count
    shard_rows = lax.all_gather(latent, "seq", axis=0, tiled=True)
    key_count = shard_rows.shape[0]
    key_index = jnp.arange(key_count, dtype=jnp.int32)
    key_segment, unused = place(key_index, lengths)
    allowed = (row_segment[:, None] == key_segment[None, :]) & (
        key_index[None, :] <= row_index[:, None]
    )
    running_max = jnp.full((row_total,), -1e30, jnp.float32)
    scores = jnp.einsum("ra,ka->rk", queries, shard_rows, preferred_element_type=jnp.float32)
    block_peak = jnp.max(jnp.where(allowed, scores, -jnp.inf), axis=1)
    new_peak = jnp.maximum(running_max, block_peak)
    weights = jnp.where(allowed, jnp.exp(scores - new_peak[:, None]), 0.0)
    running_sum = jnp.sum(weights, axis=1)
    context_sum = jnp.dot(
        weights.astype(jnp.bfloat16), shard_rows[:, :LATENT], preferred_element_type=jnp.float32
    )
    running_max, running_sum, context_sum = (new_peak, running_sum, context_sum)
    context = (context_sum / running_sum[:, None]).reshape(tok_count, head_count, LATENT)
    heads_out = jnp.einsum(
        "thc,hcv->thv",
        context,
        kv_up[:, :, NOPE:].astype(jnp.float32),
        precision=lax.Precision.HIGHEST,
    )
    heads_out = heads_out.astype(jnp.bfloat16).reshape(tok_count, head_count * VDIM)
    partial_attention = jnp.dot(heads_out, out_weight, preferred_element_type=jnp.float32)
    tp_count = lax.axis_size("tp")
    col_width = D // tp_count
    col_start = lax.axis_index("tp") * col_width
    attention_part = lax.psum_scatter(
        partial_attention.astype(jnp.bfloat16), "tp", scatter_dimension=1, tiled=True
    ).astype(jnp.float32)
    stream_part = lax.dynamic_slice_in_dim(stream, col_start, col_width, 1)
    hidden = stream_part.astype(jnp.float32) + attention_part
    square_sum = lax.psum(jnp.sum(hidden * hidden, axis=1, keepdims=True), "tp")
    gain_part = lax.dynamic_slice_in_dim(moe_gain, col_start, col_width, 0)
    normed = (hidden * lax.rsqrt(square_sum / D + 1e-06) * gain_part[None, :]).astype(jnp.bfloat16)
    experts = lax.axis_size("seq")
    top_k = routes.shape[1]
    capacity = min(tok_count, max(2, 2 * tok_count * top_k // experts))
    flat_routes = routes.reshape(-1)
    onehot = (flat_routes[:, None] == jnp.arange(experts, dtype=jnp.int32)[None, :]).astype(
        jnp.int32
    )
    slot_rank = jnp.sum((jnp.cumsum(onehot, axis=0) - onehot) * onehot, axis=1)
    slot_index = flat_routes * capacity + slot_rank
    slot_table = (
        slot_index[:, None] == jnp.arange(experts * capacity, dtype=jnp.int32)[None, :]
    ).astype(jnp.bfloat16)
    placing = jnp.sum(slot_table.reshape(tok_count, top_k, experts * capacity), axis=1)
    outgoing = jnp.einsum("ts,td->sd", placing, normed, preferred_element_type=jnp.float32).astype(
        jnp.bfloat16
    )
    outgoing = outgoing.reshape(experts, capacity, col_width)
    received = lax.all_to_all(outgoing, "seq", split_axis=0, concat_axis=0, tiled=True)
    sources, slot_count, _ = received.shape
    flat_part = received.reshape(sources * slot_count, col_width)
    flat_rows = lax.all_gather(flat_part, "tp", axis=1, tiled=True)
    gate_act = jnp.dot(flat_rows, expert_gate[0], preferred_element_type=jnp.float32)
    up_act = jnp.dot(flat_rows, expert_up[0], preferred_element_type=jnp.float32)
    hidden_units = (jax.nn.silu(gate_act) * up_act).astype(jnp.bfloat16)
    expert_out = jnp.dot(hidden_units, expert_down[0], preferred_element_type=jnp.float32).astype(
        jnp.bfloat16
    )
    expert_sum = lax.psum_scatter(expert_out, "tp", scatter_dimension=1, tiled=True)
    expert_sum = expert_sum.reshape(sources, slot_count, col_width)
    returned = lax.all_to_all(expert_sum, "seq", split_axis=0, concat_axis=0, tiled=True)
    gathered = returned.reshape(experts * capacity, col_width)[slot_index].reshape(
        tok_count, top_k, col_width
    )
    moe = jnp.zeros((tok_count, col_width), jnp.float32)
    for route_slot in range(top_k):
        moe = moe + route_weight[:, route_slot][:, None] * gathered[:, route_slot].astype(
            jnp.float32
        )
    layer_part = (hidden + moe).astype(jnp.bfloat16)
    layer_out = lax.all_gather(layer_part, "tp", axis=1, tiled=True)
    return (layer_out, latent)


def solution(mesh):
    return jax.shard_map(
        on_device,
        mesh=mesh,
        in_specs=(
            P("seq", None),
            P(),
            P(None, "tp"),
            P(),
            P(),
            P("tp", None, None),
            P("tp", None),
            P(),
            P("seq", None),
            P("seq", None),
            P("seq", None, "tp"),
            P("seq", None, "tp"),
            P("seq", "tp", None),
        ),
        out_specs=(P("seq", None), P("seq", None)),
        check_vma=False,
    )
```

```python
import jax
import jax.numpy as jnp
from jax import lax
from jax.sharding import PartitionSpec as P

D = 2048
NOPE = 128
ROPE = 64
LATENT = 512
VDIM = 128


THETA = 50000.0


def place(token_index, lengths):
    prompt_ends = jnp.cumsum(lengths)
    before = (prompt_ends[None, :] <= token_index[:, None]).astype(jnp.int32)
    segment = jnp.sum(before, axis=1)
    prompt_start = jnp.sum(before * lengths[None, :], axis=1)
    return (segment, token_index - prompt_start)


def angles(position):
    half_rope = ROPE // 2
    frequency = THETA ** (-2.0 * jnp.arange(half_rope, dtype=jnp.float32) / ROPE)
    angle_table = position.astype(jnp.float32)[:, None] * frequency[None, :]
    return (jnp.cos(angle_table), jnp.sin(angle_table))


def rotate(values, cos_table, sin_table):
    half_rope = ROPE // 2
    first_half = values[..., :half_rope]
    second = values[..., half_rope:]
    return jnp.concatenate(
        [first_half * cos_table - second * sin_table, first_half * sin_table + second * cos_table],
        axis=-1,
    )


def on_device(
    stream,
    lengths,
    q_weight,
    kv_down,
    latent_gain,
    kv_up,
    out_weight,
    moe_gain,
    routes,
    route_weight,
    expert_gate,
    expert_up,
    expert_down,
):
    tok_count = stream.shape[0]
    head_count = kv_up.shape[0]
    first_row = lax.axis_index("seq") * tok_count
    token_index = first_row + jnp.arange(tok_count, dtype=jnp.int32)
    segment, position = place(token_index, lengths)
    cos_table, sin_table = angles(position)
    kv_proj = jnp.dot(stream, kv_down, preferred_element_type=jnp.float32)
    compressed = kv_proj[:, :LATENT]
    factor = lax.rsqrt(jnp.mean(compressed * compressed, axis=1, keepdims=True) + 1e-06)
    latent = jnp.concatenate(
        [
            compressed * factor * latent_gain[None, :],
            rotate(kv_proj[:, LATENT:], cos_table, sin_table),
        ],
        axis=1,
    ).astype(jnp.bfloat16)
    q_proj = jnp.dot(stream, q_weight, preferred_element_type=jnp.float32).astype(jnp.bfloat16)
    q_proj = q_proj.reshape(tok_count, head_count, NOPE + ROPE)
    absorbed = jnp.einsum(
        "thj,hcj->thc", q_proj[:, :, :NOPE], kv_up[:, :, :NOPE], preferred_element_type=jnp.float32
    )
    rotated = rotate(
        q_proj[:, :, NOPE:].astype(jnp.float32), cos_table[:, None, :], sin_table[:, None, :]
    )
    softmax_scale = (NOPE + ROPE) ** (-0.5)
    queries = (jnp.concatenate([absorbed, rotated], axis=2) * softmax_scale).astype(jnp.bfloat16)
    queries = queries.reshape(tok_count * head_count, LATENT + ROPE)
    row_segment = jnp.repeat(segment, head_count)
    row_index = jnp.repeat(token_index, head_count)
    row_total = tok_count * head_count
    shard_rows = lax.all_gather(latent, "seq", axis=0, tiled=True)
    key_count = shard_rows.shape[0]
    key_index = jnp.arange(key_count, dtype=jnp.int32)
    key_segment, unused = place(key_index, lengths)
    allowed = (row_segment[:, None] == key_segment[None, :]) & (
        key_index[None, :] <= row_index[:, None]
    )
    running_max = jnp.full((row_total,), -1e30, jnp.float32)
    scores = jnp.einsum("ra,ka->rk", queries, shard_rows, preferred_element_type=jnp.float32)
    block_peak = jnp.max(jnp.where(allowed, scores, -jnp.inf), axis=1)
    new_peak = jnp.maximum(running_max, block_peak)
    weights = jnp.where(allowed, jnp.exp(scores - new_peak[:, None]), 0.0)
    running_sum = jnp.sum(weights, axis=1)
    context_sum = jnp.dot(
        weights.astype(jnp.bfloat16), shard_rows[:, :LATENT], preferred_element_type=jnp.float32
    )
    running_max, running_sum, context_sum = (new_peak, running_sum, context_sum)
    context = (context_sum / running_sum[:, None]).reshape(tok_count, head_count, LATENT)
    heads_out = jnp.einsum(
        "thc,hcv->thv",
        context,
        kv_up[:, :, NOPE:].astype(jnp.float32),
        precision=lax.Precision.HIGHEST,
    )
    heads_out = heads_out.astype(jnp.bfloat16).reshape(tok_count, head_count * VDIM)
    partial_attention = jnp.dot(heads_out, out_weight, preferred_element_type=jnp.float32)
    tp_count = lax.axis_size("tp")
    col_width = D // tp_count
    col_start = lax.axis_index("tp") * col_width
    attention_part = lax.psum_scatter(
        partial_attention.astype(jnp.bfloat16), "tp", scatter_dimension=1, tiled=True
    ).astype(jnp.float32)
    stream_part = lax.dynamic_slice_in_dim(stream, col_start, col_width, 1)
    hidden = stream_part.astype(jnp.float32) + attention_part
    square_sum = lax.psum(jnp.sum(hidden * hidden, axis=1, keepdims=True), "tp")
    gain_part = lax.dynamic_slice_in_dim(moe_gain, col_start, col_width, 0)
    normed = (hidden * lax.rsqrt(square_sum / D + 1e-06) * gain_part[None, :]).astype(jnp.bfloat16)
    experts = lax.axis_size("seq")
    top_k = routes.shape[1]
    capacity = min(tok_count, max(2, 2 * tok_count * top_k // experts))
    flat_routes = routes.reshape(-1)
    onehot = (flat_routes[:, None] == jnp.arange(experts, dtype=jnp.int32)[None, :]).astype(
        jnp.int32
    )
    slot_rank = jnp.sum((jnp.cumsum(onehot, axis=0) - onehot) * onehot, axis=1)
    slot_index = flat_routes * capacity + slot_rank
    slot_table = (
        slot_index[:, None] == jnp.arange(experts * capacity, dtype=jnp.int32)[None, :]
    ).astype(jnp.bfloat16)
    placing = jnp.sum(slot_table.reshape(tok_count, top_k, experts * capacity), axis=1)
    outgoing = jnp.einsum("ts,td->sd", placing, normed, preferred_element_type=jnp.float32).astype(
        jnp.bfloat16
    )
    outgoing = outgoing.reshape(experts, capacity, col_width)
    chunk_count = 2
    chunk_slots = capacity // chunk_count
    returned_chunks = []
    for chunk in range(chunk_count):
        sending = outgoing[:, chunk * chunk_slots : (chunk + 1) * chunk_slots]
        received = lax.all_to_all(sending, "seq", split_axis=0, concat_axis=0, tiled=True)
        sources, slot_count, _ = received.shape
        flat_part = received.reshape(sources * slot_count, col_width)
        flat_rows = lax.all_gather(flat_part, "tp", axis=1, tiled=True)
        gate_act = jnp.dot(flat_rows, expert_gate[0], preferred_element_type=jnp.float32)
        up_act = jnp.dot(flat_rows, expert_up[0], preferred_element_type=jnp.float32)
        hidden_units = (jax.nn.silu(gate_act) * up_act).astype(jnp.bfloat16)
        expert_out = jnp.dot(
            hidden_units, expert_down[0], preferred_element_type=jnp.float32
        ).astype(jnp.bfloat16)
        expert_sum = lax.psum_scatter(expert_out, "tp", scatter_dimension=1, tiled=True)
        expert_sum = expert_sum.reshape(sources, slot_count, col_width)
        returned_chunks.append(
            lax.all_to_all(expert_sum, "seq", split_axis=0, concat_axis=0, tiled=True)
        )
    returned = jnp.concatenate(returned_chunks, axis=1)
    gathered = returned.reshape(experts * capacity, col_width)[slot_index].reshape(
        tok_count, top_k, col_width
    )
    moe = jnp.zeros((tok_count, col_width), jnp.float32)
    for route_slot in range(top_k):
        moe = moe + route_weight[:, route_slot][:, None] * gathered[:, route_slot].astype(
            jnp.float32
        )
    layer_part = (hidden + moe).astype(jnp.bfloat16)
    layer_out = lax.all_gather(layer_part, "tp", axis=1, tiled=True)
    return (layer_out, latent)


def solution(mesh):
    return jax.shard_map(
        on_device,
        mesh=mesh,
        in_specs=(
            P("seq", None),
            P(),
            P(None, "tp"),
            P(),
            P(),
            P("tp", None, None),
            P("tp", None),
            P(),
            P("seq", None),
            P("seq", None),
            P("seq", None, "tp"),
            P("seq", None, "tp"),
            P("seq", "tp", None),
        ),
        out_specs=(P("seq", None), P("seq", None)),
        check_vma=False,
    )
```

```python
import jax
import jax.numpy as jnp
from jax import lax
from jax.sharding import PartitionSpec as P

D = 2048
NOPE = 128
ROPE = 64
LATENT = 512
VDIM = 128


THETA = 50000.0


def place(token_index, lengths):
    prompt_ends = jnp.cumsum(lengths)
    before = (prompt_ends[None, :] <= token_index[:, None]).astype(jnp.int32)
    segment = jnp.sum(before, axis=1)
    prompt_start = jnp.sum(before * lengths[None, :], axis=1)
    return (segment, token_index - prompt_start)


def angles(position):
    half_rope = ROPE // 2
    frequency = THETA ** (-2.0 * jnp.arange(half_rope, dtype=jnp.float32) / ROPE)
    angle_table = position.astype(jnp.float32)[:, None] * frequency[None, :]
    return (jnp.cos(angle_table), jnp.sin(angle_table))


def rotate(values, cos_table, sin_table):
    half_rope = ROPE // 2
    first_half = values[..., :half_rope]
    second = values[..., half_rope:]
    return jnp.concatenate(
        [first_half * cos_table - second * sin_table, first_half * sin_table + second * cos_table],
        axis=-1,
    )


def on_device(
    stream,
    lengths,
    q_weight,
    kv_down,
    latent_gain,
    kv_up,
    out_weight,
    moe_gain,
    routes,
    route_weight,
    expert_gate,
    expert_up,
    expert_down,
):
    tok_count = stream.shape[0]
    head_count = kv_up.shape[0]
    first_row = lax.axis_index("seq") * tok_count
    token_index = first_row + jnp.arange(tok_count, dtype=jnp.int32)
    segment, position = place(token_index, lengths)
    cos_table, sin_table = angles(position)
    kv_proj = jnp.dot(stream, kv_down, preferred_element_type=jnp.float32)
    compressed = kv_proj[:, :LATENT]
    factor = lax.rsqrt(jnp.mean(compressed * compressed, axis=1, keepdims=True) + 1e-06)
    latent = jnp.concatenate(
        [
            compressed * factor * latent_gain[None, :],
            rotate(kv_proj[:, LATENT:], cos_table, sin_table),
        ],
        axis=1,
    ).astype(jnp.bfloat16)
    tp_count = lax.axis_size("tp")
    tp_index = lax.axis_index("tp")
    kv_up_all = lax.all_gather(kv_up, "tp", axis=0, tiled=True)
    all_heads = kv_up_all.shape[0]
    q_proj = jnp.dot(stream, q_weight, preferred_element_type=jnp.float32).astype(jnp.bfloat16)
    q_proj = lax.all_gather(q_proj, "tp", axis=1, tiled=True)
    q_proj = q_proj.reshape(tok_count, all_heads, NOPE + ROPE)
    absorbed = jnp.einsum(
        "thj,hcj->thc", q_proj[:, :, :NOPE], kv_up_all[:, :, :NOPE], preferred_element_type=jnp.float32
    )
    rotated = rotate(
        q_proj[:, :, NOPE:].astype(jnp.float32), cos_table[:, None, :], sin_table[:, None, :]
    )
    softmax_scale = (NOPE + ROPE) ** (-0.5)
    queries = (jnp.concatenate([absorbed, rotated], axis=2) * softmax_scale).astype(jnp.bfloat16)
    queries = queries.reshape(tok_count * all_heads, LATENT + ROPE)
    row_segment = jnp.repeat(segment, all_heads)
    row_index = jnp.repeat(token_index, all_heads)
    key_rows = tok_count // tp_count
    own_keys = lax.dynamic_slice_in_dim(latent, tp_index * key_rows, key_rows, 0)
    shard_rows = lax.all_gather(own_keys, "seq", axis=0, tiled=True)
    seq_count = shard_rows.shape[0] // key_rows
    key_index = (
        jnp.arange(seq_count, dtype=jnp.int32)[:, None] * tok_count
        + tp_index * key_rows
        + jnp.arange(key_rows, dtype=jnp.int32)[None, :]
    ).reshape(-1)
    key_segment, unused = place(key_index, lengths)
    allowed = (row_segment[:, None] == key_segment[None, :]) & (
        key_index[None, :] <= row_index[:, None]
    )
    scores = jnp.einsum("ra,ka->rk", queries, shard_rows, preferred_element_type=jnp.float32)
    block_peak = jnp.max(jnp.where(allowed, scores, -jnp.inf), axis=1)
    peak = jnp.maximum(jnp.full_like(block_peak, -1e30), block_peak)
    weights = jnp.where(allowed, jnp.exp(scores - peak[:, None]), 0.0)
    weight_sum = jnp.sum(weights, axis=1)
    context_sum = jnp.dot(
        weights.astype(jnp.bfloat16), shard_rows[:, :LATENT], preferred_element_type=jnp.float32
    ).reshape(tok_count, all_heads, LATENT)
    heads_part = jnp.einsum(
        "thc,hcv->thv",
        context_sum,
        kv_up_all[:, :, NOPE:].astype(jnp.float32),
        precision=lax.Precision.HIGHEST,
    )
    packed = jnp.concatenate(
        [
            heads_part,
            weight_sum.reshape(tok_count, all_heads, 1),
            peak.reshape(tok_count, all_heads, 1),
        ],
        axis=2,
    )
    packed = packed.reshape(tok_count, tp_count, head_count, VDIM + 2).transpose(1, 0, 2, 3)
    packed = lax.all_to_all(packed, "tp", split_axis=0, concat_axis=0, tiled=True)
    part_peak = packed[:, :, :, VDIM + 1]
    top_peak = jnp.max(part_peak, axis=0)
    rescale = jnp.exp(part_peak - top_peak[None])
    numerator = jnp.sum(packed[:, :, :, :VDIM] * rescale[..., None], axis=0)
    denominator = jnp.sum(packed[:, :, :, VDIM] * rescale, axis=0)
    heads_out = numerator / denominator[..., None]
    heads_out = heads_out.astype(jnp.bfloat16).reshape(tok_count, head_count * VDIM)
    partial_attention = jnp.dot(heads_out, out_weight, preferred_element_type=jnp.float32)
    tp_count = lax.axis_size("tp")
    col_width = D // tp_count
    col_start = lax.axis_index("tp") * col_width
    attention_part = lax.psum_scatter(
        partial_attention.astype(jnp.bfloat16), "tp", scatter_dimension=1, tiled=True
    ).astype(jnp.float32)
    stream_part = lax.dynamic_slice_in_dim(stream, col_start, col_width, 1)
    hidden = stream_part.astype(jnp.float32) + attention_part
    square_sum = lax.psum(jnp.sum(hidden * hidden, axis=1, keepdims=True), "tp")
    gain_part = lax.dynamic_slice_in_dim(moe_gain, col_start, col_width, 0)
    normed = (hidden * lax.rsqrt(square_sum / D + 1e-06) * gain_part[None, :]).astype(jnp.bfloat16)
    experts = lax.axis_size("seq")
    top_k = routes.shape[1]
    capacity = min(tok_count, max(2, 2 * tok_count * top_k // experts))
    flat_routes = routes.reshape(-1)
    onehot = (flat_routes[:, None] == jnp.arange(experts, dtype=jnp.int32)[None, :]).astype(
        jnp.int32
    )
    slot_rank = jnp.sum((jnp.cumsum(onehot, axis=0) - onehot) * onehot, axis=1)
    slot_index = flat_routes * capacity + slot_rank
    slot_table = (
        slot_index[:, None] == jnp.arange(experts * capacity, dtype=jnp.int32)[None, :]
    ).astype(jnp.bfloat16)
    placing = jnp.sum(slot_table.reshape(tok_count, top_k, experts * capacity), axis=1)
    outgoing = jnp.einsum("ts,td->sd", placing, normed, preferred_element_type=jnp.float32).astype(
        jnp.bfloat16
    )
    outgoing = outgoing.reshape(experts, capacity, col_width)
    chunk_count = 2
    chunk_slots = capacity // chunk_count
    returned_chunks = []
    for chunk in range(chunk_count):
        sending = outgoing[:, chunk * chunk_slots : (chunk + 1) * chunk_slots]
        received = lax.all_to_all(sending, "seq", split_axis=0, concat_axis=0, tiled=True)
        sources, slot_count, _ = received.shape
        flat_part = received.reshape(sources * slot_count, col_width)
        flat_rows = lax.all_gather(flat_part, "tp", axis=1, tiled=True)
        gate_act = jnp.dot(flat_rows, expert_gate[0], preferred_element_type=jnp.float32)
        up_act = jnp.dot(flat_rows, expert_up[0], preferred_element_type=jnp.float32)
        hidden_units = (jax.nn.silu(gate_act) * up_act).astype(jnp.bfloat16)
        expert_out = jnp.dot(
            hidden_units, expert_down[0], preferred_element_type=jnp.float32
        ).astype(jnp.bfloat16)
        expert_sum = lax.psum_scatter(expert_out, "tp", scatter_dimension=1, tiled=True)
        expert_sum = expert_sum.reshape(sources, slot_count, col_width)
        returned_chunks.append(
            lax.all_to_all(expert_sum, "seq", split_axis=0, concat_axis=0, tiled=True)
        )
    returned = jnp.concatenate(returned_chunks, axis=1)
    gathered = returned.reshape(experts * capacity, col_width)[slot_index].reshape(
        tok_count, top_k, col_width
    )
    moe = jnp.zeros((tok_count, col_width), jnp.float32)
    for route_slot in range(top_k):
        moe = moe + route_weight[:, route_slot][:, None] * gathered[:, route_slot].astype(
            jnp.float32
        )
    layer_part = (hidden + moe).astype(jnp.bfloat16)
    layer_out = lax.all_gather(layer_part, "tp", axis=1, tiled=True)
    return (layer_out, latent)


def solution(mesh):
    return jax.shard_map(
        on_device,
        mesh=mesh,
        in_specs=(
            P("seq", None),
            P(),
            P(None, "tp"),
            P(),
            P(),
            P("tp", None, None),
            P("tp", None),
            P(),
            P("seq", None),
            P("seq", None),
            P("seq", None, "tp"),
            P("seq", None, "tp"),
            P("seq", "tp", None),
        ),
        out_specs=(P("seq", None), P("seq", None)),
        check_vma=False,
    )
```

```python
import jax
import jax.numpy as jnp
from jax import lax
from jax.experimental import pallas as pl
from jax.experimental.pallas import tpu as pltpu
from jax.sharding import PartitionSpec as P

D = 2048
NOPE = 128
ROPE = 64
LATENT = 512
VDIM = 128


THETA = 50000.0


def place(token_index, lengths):
    prompt_ends = jnp.cumsum(lengths)
    before = (prompt_ends[None, :] <= token_index[:, None]).astype(jnp.int32)
    segment = jnp.sum(before, axis=1)
    prompt_start = jnp.sum(before * lengths[None, :], axis=1)
    return (segment, token_index - prompt_start)


def angles(position):
    half_rope = ROPE // 2
    frequency = THETA ** (-2.0 * jnp.arange(half_rope, dtype=jnp.float32) / ROPE)
    angle_table = position.astype(jnp.float32)[:, None] * frequency[None, :]
    return (jnp.cos(angle_table), jnp.sin(angle_table))


def rotate(values, cos_table, sin_table):
    half_rope = ROPE // 2
    first_half = values[..., :half_rope]
    second = values[..., half_rope:]
    return jnp.concatenate(
        [first_half * cos_table - second * sin_table, first_half * sin_table + second * cos_table],
        axis=-1,
    )


def _exchange_body(x_ref, o_ref, send_sem, recv_sem, local_sem):
    n = x_ref.shape[0]
    me = lax.axis_index("seq")
    tp_me = lax.axis_index("tp")
    local = pltpu.make_async_copy(x_ref.at[me], o_ref.at[me], local_sem)
    local.start()

    def start_one(i, carry):
        dest = lax.rem(me + i, n)
        pltpu.make_async_remote_copy(
            src_ref=x_ref.at[dest],
            dst_ref=o_ref.at[me],
            send_sem=send_sem.at[dest],
            recv_sem=recv_sem.at[me],
            device_id=(dest, tp_me),
            device_id_type=pl.DeviceIdType.MESH,
        ).start()
        return carry

    lax.fori_loop(1, n, start_one, 0)

    def wait_one(i, carry):
        dest = lax.rem(me + i, n)
        source = lax.rem(me + n - i, n)
        pltpu.make_async_remote_copy(
            src_ref=x_ref.at[dest],
            dst_ref=o_ref.at[source],
            send_sem=send_sem.at[dest],
            recv_sem=recv_sem.at[source],
            device_id=(dest, tp_me),
            device_id_type=pl.DeviceIdType.MESH,
        ).wait_send()
        pltpu.make_async_remote_copy(
            src_ref=x_ref.at[source],
            dst_ref=o_ref.at[source],
            send_sem=send_sem.at[source],
            recv_sem=recv_sem.at[source],
            device_id=(source, tp_me),
            device_id_type=pl.DeviceIdType.MESH,
        ).wait_recv()
        return carry

    lax.fori_loop(1, n, wait_one, 0)
    local.wait()


def seq_exchange(x):
    n = x.shape[0]
    return pl.pallas_call(
        _exchange_body,
        out_shape=jax.ShapeDtypeStruct(x.shape, x.dtype),
        in_specs=[pl.BlockSpec(memory_space=pl.ANY)],
        out_specs=pl.BlockSpec(memory_space=pl.ANY),
        scratch_shapes=[
            pltpu.SemaphoreType.DMA((n,)),
            pltpu.SemaphoreType.DMA((n,)),
            pltpu.SemaphoreType.DMA,
        ],
        compiler_params=pltpu.CompilerParams(has_side_effects=True),
    )(x)


def on_device(
    stream,
    lengths,
    q_weight,
    kv_down,
    latent_gain,
    kv_up,
    out_weight,
    moe_gain,
    routes,
    route_weight,
    expert_gate,
    expert_up,
    expert_down,
):
    tok_count = stream.shape[0]
    head_count = kv_up.shape[0]
    first_row = lax.axis_index("seq") * tok_count
    token_index = first_row + jnp.arange(tok_count, dtype=jnp.int32)
    segment, position = place(token_index, lengths)
    cos_table, sin_table = angles(position)
    kv_proj = jnp.dot(stream, kv_down, preferred_element_type=jnp.float32)
    compressed = kv_proj[:, :LATENT]
    factor = lax.rsqrt(jnp.mean(compressed * compressed, axis=1, keepdims=True) + 1e-06)
    latent = jnp.concatenate(
        [
            compressed * factor * latent_gain[None, :],
            rotate(kv_proj[:, LATENT:], cos_table, sin_table),
        ],
        axis=1,
    ).astype(jnp.bfloat16)
    q_proj = jnp.dot(stream, q_weight, preferred_element_type=jnp.float32).astype(jnp.bfloat16)
    q_proj = q_proj.reshape(tok_count, head_count, NOPE + ROPE)
    absorbed = jnp.einsum(
        "thj,hcj->thc", q_proj[:, :, :NOPE], kv_up[:, :, :NOPE], preferred_element_type=jnp.float32
    )
    rotated = rotate(
        q_proj[:, :, NOPE:].astype(jnp.float32), cos_table[:, None, :], sin_table[:, None, :]
    )
    softmax_scale = (NOPE + ROPE) ** (-0.5)
    queries = (jnp.concatenate([absorbed, rotated], axis=2) * softmax_scale).astype(jnp.bfloat16)
    queries = queries.reshape(tok_count * head_count, LATENT + ROPE)
    row_segment = jnp.repeat(segment, head_count)
    row_index = jnp.repeat(token_index, head_count)
    row_total = tok_count * head_count
    shard_rows = lax.all_gather(latent, "seq", axis=0, tiled=True)
    key_count = shard_rows.shape[0]
    key_index = jnp.arange(key_count, dtype=jnp.int32)
    key_segment, unused = place(key_index, lengths)
    allowed = (row_segment[:, None] == key_segment[None, :]) & (
        key_index[None, :] <= row_index[:, None]
    )
    running_max = jnp.full((row_total,), -1e30, jnp.float32)
    scores = jnp.einsum("ra,ka->rk", queries, shard_rows, preferred_element_type=jnp.float32)
    block_peak = jnp.max(jnp.where(allowed, scores, -jnp.inf), axis=1)
    new_peak = jnp.maximum(running_max, block_peak)
    weights = jnp.where(allowed, jnp.exp(scores - new_peak[:, None]), 0.0)
    running_sum = jnp.sum(weights, axis=1)
    context_sum = jnp.dot(
        weights.astype(jnp.bfloat16), shard_rows[:, :LATENT], preferred_element_type=jnp.float32
    )
    running_max, running_sum, context_sum = (new_peak, running_sum, context_sum)
    context = (context_sum / running_sum[:, None]).reshape(tok_count, head_count, LATENT)
    heads_out = jnp.einsum(
        "thc,hcv->thv",
        context,
        kv_up[:, :, NOPE:].astype(jnp.float32),
        precision=lax.Precision.HIGHEST,
    )
    heads_out = heads_out.astype(jnp.bfloat16).reshape(tok_count, head_count * VDIM)
    partial_attention = jnp.dot(heads_out, out_weight, preferred_element_type=jnp.float32)
    tp_count = lax.axis_size("tp")
    col_width = D // tp_count
    col_start = lax.axis_index("tp") * col_width
    attention_part = lax.psum_scatter(
        partial_attention.astype(jnp.bfloat16), "tp", scatter_dimension=1, tiled=True
    ).astype(jnp.float32)
    stream_part = lax.dynamic_slice_in_dim(stream, col_start, col_width, 1)
    hidden = stream_part.astype(jnp.float32) + attention_part
    square_sum = lax.psum(jnp.sum(hidden * hidden, axis=1, keepdims=True), "tp")
    gain_part = lax.dynamic_slice_in_dim(moe_gain, col_start, col_width, 0)
    normed = (hidden * lax.rsqrt(square_sum / D + 1e-06) * gain_part[None, :]).astype(jnp.bfloat16)
    experts = lax.axis_size("seq")
    top_k = routes.shape[1]
    capacity = min(tok_count, max(2, 2 * tok_count * top_k // experts))
    flat_routes = routes.reshape(-1)
    onehot = (flat_routes[:, None] == jnp.arange(experts, dtype=jnp.int32)[None, :]).astype(
        jnp.int32
    )
    slot_rank = jnp.sum((jnp.cumsum(onehot, axis=0) - onehot) * onehot, axis=1)
    slot_index = flat_routes * capacity + slot_rank
    slot_table = (
        slot_index[:, None] == jnp.arange(experts * capacity, dtype=jnp.int32)[None, :]
    ).astype(jnp.bfloat16)
    placing = jnp.sum(slot_table.reshape(tok_count, top_k, experts * capacity), axis=1)
    outgoing = jnp.einsum("ts,td->sd", placing, normed, preferred_element_type=jnp.float32).astype(
        jnp.bfloat16
    )
    outgoing = outgoing.reshape(experts, capacity, col_width)
    chunk_count = 2
    chunk_slots = capacity // chunk_count
    returned_chunks = []
    for chunk in range(chunk_count):
        sending = outgoing[:, chunk * chunk_slots : (chunk + 1) * chunk_slots]
        received = seq_exchange(sending)
        sources, slot_count, _ = received.shape
        flat_part = received.reshape(sources * slot_count, col_width)
        flat_rows = lax.all_gather(flat_part, "tp", axis=1, tiled=True)
        gate_act = jnp.dot(flat_rows, expert_gate[0], preferred_element_type=jnp.float32)
        up_act = jnp.dot(flat_rows, expert_up[0], preferred_element_type=jnp.float32)
        hidden_units = (jax.nn.silu(gate_act) * up_act).astype(jnp.bfloat16)
        expert_out = jnp.dot(
            hidden_units, expert_down[0], preferred_element_type=jnp.float32
        ).astype(jnp.bfloat16)
        expert_sum = lax.psum_scatter(expert_out, "tp", scatter_dimension=1, tiled=True)
        expert_sum = expert_sum.reshape(sources, slot_count, col_width)
        returned_chunks.append(
            seq_exchange(expert_sum)
        )
    returned = jnp.concatenate(returned_chunks, axis=1)
    gathered = returned.reshape(experts * capacity, col_width)[slot_index].reshape(
        tok_count, top_k, col_width
    )
    moe = jnp.zeros((tok_count, col_width), jnp.float32)
    for route_slot in range(top_k):
        moe = moe + route_weight[:, route_slot][:, None] * gathered[:, route_slot].astype(
            jnp.float32
        )
    layer_part = (hidden + moe).astype(jnp.bfloat16)
    layer_out = lax.all_gather(layer_part, "tp", axis=1, tiled=True)
    return (layer_out, latent)


def solution(mesh):
    return jax.shard_map(
        on_device,
        mesh=mesh,
        in_specs=(
            P("seq", None),
            P(),
            P(None, "tp"),
            P(),
            P(),
            P("tp", None, None),
            P("tp", None),
            P(),
            P("seq", None),
            P("seq", None),
            P("seq", None, "tp"),
            P("seq", None, "tp"),
            P("seq", "tp", None),
        ),
        out_specs=(P("seq", None), P("seq", None)),
        check_vma=False,
    )
```

```python
import jax
import jax.numpy as jnp
from jax import lax
from jax.experimental import pallas as pl
from jax.experimental.pallas import tpu as pltpu
from jax.sharding import PartitionSpec as P

D = 2048
NOPE = 128
ROPE = 64
LATENT = 512
VDIM = 128


THETA = 50000.0


def place(token_index, lengths):
    prompt_ends = jnp.cumsum(lengths)
    before = (prompt_ends[None, :] <= token_index[:, None]).astype(jnp.int32)
    segment = jnp.sum(before, axis=1)
    prompt_start = jnp.sum(before * lengths[None, :], axis=1)
    return (segment, token_index - prompt_start)


def angles(position):
    half_rope = ROPE // 2
    frequency = THETA ** (-2.0 * jnp.arange(half_rope, dtype=jnp.float32) / ROPE)
    angle_table = position.astype(jnp.float32)[:, None] * frequency[None, :]
    return (jnp.cos(angle_table), jnp.sin(angle_table))


def rotate(values, cos_table, sin_table):
    half_rope = ROPE // 2
    first_half = values[..., :half_rope]
    second = values[..., half_rope:]
    return jnp.concatenate(
        [first_half * cos_table - second * sin_table, first_half * sin_table + second * cos_table],
        axis=-1,
    )


def _exchange_body(x_ref, o_ref, send_sem, recv_sem, local_sem):
    n = x_ref.shape[0]
    me = lax.axis_index("seq")
    tp_me = lax.axis_index("tp")
    local = pltpu.make_async_copy(x_ref.at[me], o_ref.at[me], local_sem)
    local.start()

    def start_one(i, carry):
        dest = lax.rem(me + i, n)
        pltpu.make_async_remote_copy(
            src_ref=x_ref.at[dest],
            dst_ref=o_ref.at[me],
            send_sem=send_sem.at[dest],
            recv_sem=recv_sem.at[me],
            device_id=(dest, tp_me),
            device_id_type=pl.DeviceIdType.MESH,
        ).start()
        return carry

    lax.fori_loop(1, n, start_one, 0)

    def wait_one(i, carry):
        dest = lax.rem(me + i, n)
        source = lax.rem(me + n - i, n)
        pltpu.make_async_remote_copy(
            src_ref=x_ref.at[dest],
            dst_ref=o_ref.at[source],
            send_sem=send_sem.at[dest],
            recv_sem=recv_sem.at[source],
            device_id=(dest, tp_me),
            device_id_type=pl.DeviceIdType.MESH,
        ).wait_send()
        pltpu.make_async_remote_copy(
            src_ref=x_ref.at[source],
            dst_ref=o_ref.at[source],
            send_sem=send_sem.at[source],
            recv_sem=recv_sem.at[source],
            device_id=(source, tp_me),
            device_id_type=pl.DeviceIdType.MESH,
        ).wait_recv()
        return carry

    lax.fori_loop(1, n, wait_one, 0)
    local.wait()


def seq_exchange(x):
    n = x.shape[0]
    return pl.pallas_call(
        _exchange_body,
        out_shape=jax.ShapeDtypeStruct(x.shape, x.dtype),
        in_specs=[pl.BlockSpec(memory_space=pl.ANY)],
        out_specs=pl.BlockSpec(memory_space=pl.ANY),
        scratch_shapes=[
            pltpu.SemaphoreType.DMA((n,)),
            pltpu.SemaphoreType.DMA((n,)),
            pltpu.SemaphoreType.DMA,
        ],
        compiler_params=pltpu.CompilerParams(has_side_effects=True),
    )(x)


def on_device(
    stream,
    lengths,
    q_weight,
    kv_down,
    latent_gain,
    kv_up,
    out_weight,
    moe_gain,
    routes,
    route_weight,
    expert_gate,
    expert_up,
    expert_down,
):
    tok_count = stream.shape[0]
    head_count = kv_up.shape[0]
    first_row = lax.axis_index("seq") * tok_count
    token_index = first_row + jnp.arange(tok_count, dtype=jnp.int32)
    segment, position = place(token_index, lengths)
    cos_table, sin_table = angles(position)
    kv_proj = jnp.dot(stream, kv_down, preferred_element_type=jnp.float32)
    compressed = kv_proj[:, :LATENT]
    factor = lax.rsqrt(jnp.mean(compressed * compressed, axis=1, keepdims=True) + 1e-06)
    latent = jnp.concatenate(
        [
            compressed * factor * latent_gain[None, :],
            rotate(kv_proj[:, LATENT:], cos_table, sin_table),
        ],
        axis=1,
    ).astype(jnp.bfloat16)
    q_proj = jnp.dot(stream, q_weight, preferred_element_type=jnp.float32).astype(jnp.bfloat16)
    q_proj = q_proj.reshape(tok_count, head_count, NOPE + ROPE)
    absorbed = jnp.einsum(
        "thj,hcj->thc", q_proj[:, :, :NOPE], kv_up[:, :, :NOPE], preferred_element_type=jnp.float32
    )
    rotated = rotate(
        q_proj[:, :, NOPE:].astype(jnp.float32), cos_table[:, None, :], sin_table[:, None, :]
    )
    softmax_scale = (NOPE + ROPE) ** (-0.5)
    queries = (jnp.concatenate([absorbed, rotated], axis=2) * softmax_scale).astype(jnp.bfloat16)
    queries = queries.reshape(tok_count * head_count, LATENT + ROPE)
    row_segment = jnp.repeat(segment, head_count)
    row_index = jnp.repeat(token_index, head_count)
    row_total = tok_count * head_count
    shard_rows = lax.all_gather(latent, "seq", axis=0, tiled=True)
    key_count = shard_rows.shape[0]
    key_index = jnp.arange(key_count, dtype=jnp.int32)
    key_segment, unused = place(key_index, lengths)
    allowed = (row_segment[:, None] == key_segment[None, :]) & (
        key_index[None, :] <= row_index[:, None]
    )
    running_max = jnp.full((row_total,), -1e30, jnp.float32)
    scores = jnp.einsum("ra,ka->rk", queries, shard_rows, preferred_element_type=jnp.float32)
    block_peak = jnp.max(jnp.where(allowed, scores, -jnp.inf), axis=1)
    new_peak = jnp.maximum(running_max, block_peak)
    weights = jnp.where(allowed, jnp.exp(scores - new_peak[:, None]), 0.0)
    running_sum = jnp.sum(weights, axis=1)
    context_sum = jnp.dot(
        weights.astype(jnp.bfloat16), shard_rows[:, :LATENT], preferred_element_type=jnp.float32
    )
    running_max, running_sum, context_sum = (new_peak, running_sum, context_sum)
    context = (context_sum / running_sum[:, None]).reshape(tok_count, head_count, LATENT)
    heads_out = jnp.einsum(
        "thc,hcv->thv",
        context,
        kv_up[:, :, NOPE:].astype(jnp.float32),
        precision=lax.Precision.HIGHEST,
    )
    heads_out = heads_out.astype(jnp.bfloat16).reshape(tok_count, head_count * VDIM)
    partial_attention = jnp.dot(heads_out, out_weight, preferred_element_type=jnp.float32)
    tp_count = lax.axis_size("tp")
    col_width = D // tp_count
    col_start = lax.axis_index("tp") * col_width
    attention_part = lax.psum_scatter(
        partial_attention.astype(jnp.bfloat16), "tp", scatter_dimension=1, tiled=True
    ).astype(jnp.float32)
    stream_part = lax.dynamic_slice_in_dim(stream, col_start, col_width, 1)
    hidden = stream_part.astype(jnp.float32) + attention_part
    square_sum = lax.psum(jnp.sum(hidden * hidden, axis=1, keepdims=True), "tp")
    gain_part = lax.dynamic_slice_in_dim(moe_gain, col_start, col_width, 0)
    normed = (hidden * lax.rsqrt(square_sum / D + 1e-06) * gain_part[None, :]).astype(jnp.bfloat16)
    experts = lax.axis_size("seq")
    top_k = routes.shape[1]
    capacity = min(tok_count, max(2, 2 * tok_count * top_k // experts))
    flat_routes = routes.reshape(-1)
    onehot = (flat_routes[:, None] == jnp.arange(experts, dtype=jnp.int32)[None, :]).astype(
        jnp.int32
    )
    slot_rank = jnp.sum((jnp.cumsum(onehot, axis=0) - onehot) * onehot, axis=1)
    slot_index = flat_routes * capacity + slot_rank
    slot_table = (
        slot_index[:, None] == jnp.arange(experts * capacity, dtype=jnp.int32)[None, :]
    ).astype(jnp.bfloat16)
    placing = jnp.sum(slot_table.reshape(tok_count, top_k, experts * capacity), axis=1)
    outgoing = jnp.einsum("ts,td->sd", placing, normed, preferred_element_type=jnp.float32).astype(
        jnp.bfloat16
    )
    outgoing = outgoing.reshape(experts, capacity, col_width)
    received = seq_exchange(outgoing)
    sources, slot_count, _ = received.shape
    flat_part = received.reshape(sources * slot_count, col_width)
    flat_rows = lax.all_gather(flat_part, "tp", axis=1, tiled=True)
    gate_act = jnp.dot(flat_rows, expert_gate[0], preferred_element_type=jnp.float32)
    up_act = jnp.dot(flat_rows, expert_up[0], preferred_element_type=jnp.float32)
    hidden_units = (jax.nn.silu(gate_act) * up_act).astype(jnp.bfloat16)
    expert_out = jnp.dot(hidden_units, expert_down[0], preferred_element_type=jnp.float32).astype(
        jnp.bfloat16
    )
    expert_sum = lax.psum_scatter(expert_out, "tp", scatter_dimension=1, tiled=True)
    expert_sum = expert_sum.reshape(sources, slot_count, col_width)
    returned = seq_exchange(expert_sum)
    gathered = returned.reshape(experts * capacity, col_width)[slot_index].reshape(
        tok_count, top_k, col_width
    )
    moe = jnp.zeros((tok_count, col_width), jnp.float32)
    for route_slot in range(top_k):
        moe = moe + route_weight[:, route_slot][:, None] * gathered[:, route_slot].astype(
            jnp.float32
        )
    layer_part = (hidden + moe).astype(jnp.bfloat16)
    layer_out = lax.all_gather(layer_part, "tp", axis=1, tiled=True)
    return (layer_out, latent)


def solution(mesh):
    return jax.shard_map(
        on_device,
        mesh=mesh,
        in_specs=(
            P("seq", None),
            P(),
            P(None, "tp"),
            P(),
            P(),
            P("tp", None, None),
            P("tp", None),
            P(),
            P("seq", None),
            P("seq", None),
            P("seq", None, "tp"),
            P("seq", None, "tp"),
            P("seq", "tp", None),
        ),
        out_specs=(P("seq", None), P("seq", None)),
        check_vma=False,
    )
```

```python
import jax
import jax.numpy as jnp
from jax import lax
from jax.sharding import PartitionSpec as P

D = 2048
NOPE = 128
ROPE = 64
LATENT = 512
VDIM = 128


THETA = 50000.0


def place(token_index, lengths):
    prompt_ends = jnp.cumsum(lengths)
    before = (prompt_ends[None, :] <= token_index[:, None]).astype(jnp.int32)
    segment = jnp.sum(before, axis=1)
    prompt_start = jnp.sum(before * lengths[None, :], axis=1)
    return (segment, token_index - prompt_start)


def angles(position):
    half_rope = ROPE // 2
    frequency = THETA ** (-2.0 * jnp.arange(half_rope, dtype=jnp.float32) / ROPE)
    angle_table = position.astype(jnp.float32)[:, None] * frequency[None, :]
    return (jnp.cos(angle_table), jnp.sin(angle_table))


def rotate(values, cos_table, sin_table):
    half_rope = ROPE // 2
    first_half = values[..., :half_rope]
    second = values[..., half_rope:]
    return jnp.concatenate(
        [first_half * cos_table - second * sin_table, first_half * sin_table + second * cos_table],
        axis=-1,
    )


def on_device(
    stream,
    lengths,
    q_weight,
    kv_down,
    latent_gain,
    kv_up,
    out_weight,
    moe_gain,
    routes,
    route_weight,
    expert_gate,
    expert_up,
    expert_down,
):
    tok_count = stream.shape[0]
    head_count = kv_up.shape[0]
    first_row = lax.axis_index("seq") * tok_count
    token_index = first_row + jnp.arange(tok_count, dtype=jnp.int32)
    segment, position = place(token_index, lengths)
    cos_table, sin_table = angles(position)
    kv_proj = jnp.dot(stream, kv_down, preferred_element_type=jnp.float32)
    compressed = kv_proj[:, :LATENT]
    factor = lax.rsqrt(jnp.mean(compressed * compressed, axis=1, keepdims=True) + 1e-06)
    latent = jnp.concatenate(
        [
            compressed * factor * latent_gain[None, :],
            rotate(kv_proj[:, LATENT:], cos_table, sin_table),
        ],
        axis=1,
    ).astype(jnp.bfloat16)
    q_proj = jnp.dot(stream, q_weight, preferred_element_type=jnp.float32).astype(jnp.bfloat16)
    q_proj = q_proj.reshape(tok_count, head_count, NOPE + ROPE)
    absorbed = jnp.einsum(
        "thj,hcj->thc", q_proj[:, :, :NOPE], kv_up[:, :, :NOPE], preferred_element_type=jnp.float32
    )
    rotated = rotate(
        q_proj[:, :, NOPE:].astype(jnp.float32), cos_table[:, None, :], sin_table[:, None, :]
    )
    softmax_scale = (NOPE + ROPE) ** (-0.5)
    queries = (jnp.concatenate([absorbed, rotated], axis=2) * softmax_scale).astype(jnp.bfloat16)
    queries = queries.reshape(tok_count * head_count, LATENT + ROPE)
    row_segment = jnp.repeat(segment, head_count)
    row_index = jnp.repeat(token_index, head_count)
    row_total = tok_count * head_count
    quarter_rows = tok_count // lax.axis_size("tp")
    own_rows = lax.dynamic_slice_in_dim(latent, lax.axis_index("tp") * quarter_rows, quarter_rows, 0)
    shard_rows = lax.all_gather(own_rows, ("seq", "tp"), axis=0, tiled=True)
    key_count = shard_rows.shape[0]
    key_index = jnp.arange(key_count, dtype=jnp.int32)
    key_segment, unused = place(key_index, lengths)
    allowed = (row_segment[:, None] == key_segment[None, :]) & (
        key_index[None, :] <= row_index[:, None]
    )
    running_max = jnp.full((row_total,), -1e30, jnp.float32)
    scores = jnp.einsum("ra,ka->rk", queries, shard_rows, preferred_element_type=jnp.float32)
    block_peak = jnp.max(jnp.where(allowed, scores, -jnp.inf), axis=1)
    new_peak = jnp.maximum(running_max, block_peak)
    weights = jnp.where(allowed, jnp.exp(scores - new_peak[:, None]), 0.0)
    running_sum = jnp.sum(weights, axis=1)
    context_sum = jnp.dot(
        weights.astype(jnp.bfloat16), shard_rows[:, :LATENT], preferred_element_type=jnp.float32
    )
    running_max, running_sum, context_sum = (new_peak, running_sum, context_sum)
    context = (context_sum / running_sum[:, None]).reshape(tok_count, head_count, LATENT)
    heads_out = jnp.einsum(
        "thc,hcv->thv",
        context,
        kv_up[:, :, NOPE:].astype(jnp.float32),
        precision=lax.Precision.HIGHEST,
    )
    heads_out = heads_out.astype(jnp.bfloat16).reshape(tok_count, head_count * VDIM)
    partial_attention = jnp.dot(heads_out, out_weight, preferred_element_type=jnp.float32)
    tp_count = lax.axis_size("tp")
    col_width = D // tp_count
    col_start = lax.axis_index("tp") * col_width
    attention_part = lax.psum_scatter(
        partial_attention.astype(jnp.bfloat16), "tp", scatter_dimension=1, tiled=True
    ).astype(jnp.float32)
    stream_part = lax.dynamic_slice_in_dim(stream, col_start, col_width, 1)
    hidden = stream_part.astype(jnp.float32) + attention_part
    square_sum = lax.psum(jnp.sum(hidden * hidden, axis=1, keepdims=True), "tp")
    gain_part = lax.dynamic_slice_in_dim(moe_gain, col_start, col_width, 0)
    normed = (hidden * lax.rsqrt(square_sum / D + 1e-06) * gain_part[None, :]).astype(jnp.bfloat16)
    experts = lax.axis_size("seq")
    top_k = routes.shape[1]
    capacity = min(tok_count, max(2, 2 * tok_count * top_k // experts))
    flat_routes = routes.reshape(-1)
    onehot = (flat_routes[:, None] == jnp.arange(experts, dtype=jnp.int32)[None, :]).astype(
        jnp.int32
    )
    slot_rank = jnp.sum((jnp.cumsum(onehot, axis=0) - onehot) * onehot, axis=1)
    slot_index = flat_routes * capacity + slot_rank
    slot_table = (
        slot_index[:, None] == jnp.arange(experts * capacity, dtype=jnp.int32)[None, :]
    ).astype(jnp.bfloat16)
    placing = jnp.sum(slot_table.reshape(tok_count, top_k, experts * capacity), axis=1)
    outgoing = jnp.einsum("ts,td->sd", placing, normed, preferred_element_type=jnp.float32).astype(
        jnp.bfloat16
    )
    outgoing = outgoing.reshape(experts, capacity, col_width)
    chunk_count = 2
    chunk_slots = capacity // chunk_count
    returned_chunks = []
    for chunk in range(chunk_count):
        sending = outgoing[:, chunk * chunk_slots : (chunk + 1) * chunk_slots]
        received = lax.all_to_all(sending, "seq", split_axis=0, concat_axis=0, tiled=True)
        sources, slot_count, _ = received.shape
        flat_part = received.reshape(sources * slot_count, col_width)
        flat_rows = lax.all_gather(flat_part, "tp", axis=1, tiled=True)
        gate_act = jnp.dot(flat_rows, expert_gate[0], preferred_element_type=jnp.float32)
        up_act = jnp.dot(flat_rows, expert_up[0], preferred_element_type=jnp.float32)
        hidden_units = (jax.nn.silu(gate_act) * up_act).astype(jnp.bfloat16)
        expert_out = jnp.dot(
            hidden_units, expert_down[0], preferred_element_type=jnp.float32
        ).astype(jnp.bfloat16)
        expert_sum = lax.psum_scatter(expert_out, "tp", scatter_dimension=1, tiled=True)
        expert_sum = expert_sum.reshape(sources, slot_count, col_width)
        returned_chunks.append(
            lax.all_to_all(expert_sum, "seq", split_axis=0, concat_axis=0, tiled=True)
        )
    returned = jnp.concatenate(returned_chunks, axis=1)
    gathered = returned.reshape(experts * capacity, col_width)[slot_index].reshape(
        tok_count, top_k, col_width
    )
    moe = jnp.zeros((tok_count, col_width), jnp.float32)
    for route_slot in range(top_k):
        moe = moe + route_weight[:, route_slot][:, None] * gathered[:, route_slot].astype(
            jnp.float32
        )
    layer_part = (hidden + moe).astype(jnp.bfloat16)
    layer_out = lax.all_gather(layer_part, "tp", axis=1, tiled=True)
    return (layer_out, latent)


def solution(mesh):
    return jax.shard_map(
        on_device,
        mesh=mesh,
        in_specs=(
            P("seq", None),
            P(),
            P(None, "tp"),
            P(),
            P(),
            P("tp", None, None),
            P("tp", None),
            P(),
            P("seq", None),
            P("seq", None),
            P("seq", None, "tp"),
            P("seq", None, "tp"),
            P("seq", "tp", None),
        ),
        out_specs=(P("seq", None), P("seq", None)),
        check_vma=False,
    )
```

```python
import jax
import jax.numpy as jnp
from jax import lax
from jax.sharding import PartitionSpec as P

D = 2048
NOPE = 128
ROPE = 64
LATENT = 512
VDIM = 128


THETA = 50000.0


def place(token_index, lengths):
    prompt_ends = jnp.cumsum(lengths)
    before = (prompt_ends[None, :] <= token_index[:, None]).astype(jnp.int32)
    segment = jnp.sum(before, axis=1)
    prompt_start = jnp.sum(before * lengths[None, :], axis=1)
    return (segment, token_index - prompt_start)


def angles(position):
    half_rope = ROPE // 2
    frequency = THETA ** (-2.0 * jnp.arange(half_rope, dtype=jnp.float32) / ROPE)
    angle_table = position.astype(jnp.float32)[:, None] * frequency[None, :]
    return (jnp.cos(angle_table), jnp.sin(angle_table))


def rotate(values, cos_table, sin_table):
    half_rope = ROPE // 2
    first_half = values[..., :half_rope]
    second = values[..., half_rope:]
    return jnp.concatenate(
        [first_half * cos_table - second * sin_table, first_half * sin_table + second * cos_table],
        axis=-1,
    )


def on_device(
    stream,
    lengths,
    q_weight,
    kv_down,
    latent_gain,
    kv_up,
    out_weight,
    moe_gain,
    routes,
    route_weight,
    expert_gate,
    expert_up,
    expert_down,
):
    tok_count = stream.shape[0]
    head_count = kv_up.shape[0]
    first_row = lax.axis_index("seq") * tok_count
    token_index = first_row + jnp.arange(tok_count, dtype=jnp.int32)
    segment, position = place(token_index, lengths)
    cos_table, sin_table = angles(position)
    kv_proj = jnp.dot(stream, kv_down, preferred_element_type=jnp.float32)
    compressed = kv_proj[:, :LATENT]
    factor = lax.rsqrt(jnp.mean(compressed * compressed, axis=1, keepdims=True) + 1e-06)
    latent = jnp.concatenate(
        [
            compressed * factor * latent_gain[None, :],
            rotate(kv_proj[:, LATENT:], cos_table, sin_table),
        ],
        axis=1,
    ).astype(jnp.bfloat16)
    q_proj = jnp.dot(stream, q_weight, preferred_element_type=jnp.float32).astype(jnp.bfloat16)
    q_proj = q_proj.reshape(tok_count, head_count, NOPE + ROPE)
    absorbed = jnp.einsum(
        "thj,hcj->thc", q_proj[:, :, :NOPE], kv_up[:, :, :NOPE], preferred_element_type=jnp.float32
    )
    rotated = rotate(
        q_proj[:, :, NOPE:].astype(jnp.float32), cos_table[:, None, :], sin_table[:, None, :]
    )
    softmax_scale = (NOPE + ROPE) ** (-0.5)
    queries = (jnp.concatenate([absorbed, rotated], axis=2) * softmax_scale).astype(jnp.bfloat16)
    queries = queries.reshape(tok_count * head_count, LATENT + ROPE)
    row_segment = jnp.repeat(segment, head_count)
    row_index = jnp.repeat(token_index, head_count)
    row_total = tok_count * head_count
    shard_rows = lax.all_gather(latent, "seq", axis=0, tiled=True)
    key_count = shard_rows.shape[0]
    key_index = jnp.arange(key_count, dtype=jnp.int32)
    key_segment, unused = place(key_index, lengths)
    allowed = (row_segment[:, None] == key_segment[None, :]) & (
        key_index[None, :] <= row_index[:, None]
    )
    running_max = jnp.full((row_total,), -1e30, jnp.float32)
    scores = jnp.einsum("ra,ka->rk", queries, shard_rows, preferred_element_type=jnp.float32)
    block_peak = jnp.max(jnp.where(allowed, scores, -jnp.inf), axis=1)
    new_peak = jnp.maximum(running_max, block_peak)
    weights = jnp.where(allowed, jnp.exp(scores - new_peak[:, None]), 0.0)
    running_sum = jnp.sum(weights, axis=1)
    context_sum = jnp.dot(
        weights.astype(jnp.bfloat16), shard_rows[:, :LATENT], preferred_element_type=jnp.float32
    )
    running_max, running_sum, context_sum = (new_peak, running_sum, context_sum)
    context = (context_sum / running_sum[:, None]).reshape(tok_count, head_count, LATENT)
    heads_out = jnp.einsum(
        "thc,hcv->thv",
        context,
        kv_up[:, :, NOPE:].astype(jnp.float32),
        precision=lax.Precision.HIGHEST,
    )
    heads_out = heads_out.astype(jnp.bfloat16).reshape(tok_count, head_count * VDIM)
    partial_attention = jnp.dot(heads_out, out_weight, preferred_element_type=jnp.float32)
    tp_count = lax.axis_size("tp")
    col_width = D // tp_count
    col_start = lax.axis_index("tp") * col_width
    attention_part = lax.psum_scatter(
        partial_attention.astype(jnp.bfloat16), "tp", scatter_dimension=1, tiled=True
    ).astype(jnp.float32)
    stream_part = lax.dynamic_slice_in_dim(stream, col_start, col_width, 1)
    hidden = stream_part.astype(jnp.float32) + attention_part
    normed = hidden.astype(jnp.bfloat16)
    experts = lax.axis_size("seq")
    top_k = routes.shape[1]
    capacity = min(tok_count, max(2, 2 * tok_count * top_k // experts))
    flat_routes = routes.reshape(-1)
    onehot = (flat_routes[:, None] == jnp.arange(experts, dtype=jnp.int32)[None, :]).astype(
        jnp.int32
    )
    slot_rank = jnp.sum((jnp.cumsum(onehot, axis=0) - onehot) * onehot, axis=1)
    slot_index = flat_routes * capacity + slot_rank
    slot_table = (
        slot_index[:, None] == jnp.arange(experts * capacity, dtype=jnp.int32)[None, :]
    ).astype(jnp.bfloat16)
    placing = jnp.sum(slot_table.reshape(tok_count, top_k, experts * capacity), axis=1)
    outgoing = jnp.einsum("ts,td->sd", placing, normed, preferred_element_type=jnp.float32).astype(
        jnp.bfloat16
    )
    outgoing = outgoing.reshape(experts, capacity, col_width)
    chunk_count = 2
    chunk_slots = capacity // chunk_count
    returned_chunks = []
    for chunk in range(chunk_count):
        sending = outgoing[:, chunk * chunk_slots : (chunk + 1) * chunk_slots]
        received = lax.all_to_all(sending, "seq", split_axis=0, concat_axis=0, tiled=True)
        sources, slot_count, _ = received.shape
        flat_part = received.reshape(sources * slot_count, col_width)
        flat_rows = lax.all_gather(flat_part, "tp", axis=1, tiled=True).astype(jnp.float32)
        flat_rows = (
            flat_rows
            * lax.rsqrt(jnp.mean(flat_rows * flat_rows, axis=1, keepdims=True) + 1e-06)
            * moe_gain[None, :]
        ).astype(jnp.bfloat16)
        gate_act = jnp.dot(flat_rows, expert_gate[0], preferred_element_type=jnp.float32)
        up_act = jnp.dot(flat_rows, expert_up[0], preferred_element_type=jnp.float32)
        hidden_units = (jax.nn.silu(gate_act) * up_act).astype(jnp.bfloat16)
        expert_out = jnp.dot(
            hidden_units, expert_down[0], preferred_element_type=jnp.float32
        ).astype(jnp.bfloat16)
        expert_sum = lax.psum_scatter(expert_out, "tp", scatter_dimension=1, tiled=True)
        expert_sum = expert_sum.reshape(sources, slot_count, col_width)
        returned_chunks.append(
            lax.all_to_all(expert_sum, "seq", split_axis=0, concat_axis=0, tiled=True)
        )
    returned = jnp.concatenate(returned_chunks, axis=1)
    gathered = returned.reshape(experts * capacity, col_width)[slot_index].reshape(
        tok_count, top_k, col_width
    )
    moe = jnp.zeros((tok_count, col_width), jnp.float32)
    for route_slot in range(top_k):
        moe = moe + route_weight[:, route_slot][:, None] * gathered[:, route_slot].astype(
            jnp.float32
        )
    layer_part = (hidden + moe).astype(jnp.bfloat16)
    layer_out = lax.all_gather(layer_part, "tp", axis=1, tiled=True)
    return (layer_out, latent)


def solution(mesh):
    return jax.shard_map(
        on_device,
        mesh=mesh,
        in_specs=(
            P("seq", None),
            P(),
            P(None, "tp"),
            P(),
            P(),
            P("tp", None, None),
            P("tp", None),
            P(),
            P("seq", None),
            P("seq", None),
            P("seq", None, "tp"),
            P("seq", None, "tp"),
            P("seq", "tp", None),
        ),
        out_specs=(P("seq", None), P("seq", None)),
        check_vma=False,
    )
```

```python
import jax
import jax.numpy as jnp
from jax import lax
from jax.sharding import PartitionSpec as P

D = 2048
NOPE = 128
ROPE = 64
LATENT = 512
VDIM = 128


THETA = 50000.0


def place(token_index, lengths):
    prompt_ends = jnp.cumsum(lengths)
    before = (prompt_ends[None, :] <= token_index[:, None]).astype(jnp.int32)
    segment = jnp.sum(before, axis=1)
    prompt_start = jnp.sum(before * lengths[None, :], axis=1)
    return (segment, token_index - prompt_start)


def angles(position):
    half_rope = ROPE // 2
    frequency = THETA ** (-2.0 * jnp.arange(half_rope, dtype=jnp.float32) / ROPE)
    angle_table = position.astype(jnp.float32)[:, None] * frequency[None, :]
    return (jnp.cos(angle_table), jnp.sin(angle_table))


def rotate(values, cos_table, sin_table):
    half_rope = ROPE // 2
    first_half = values[..., :half_rope]
    second = values[..., half_rope:]
    return jnp.concatenate(
        [first_half * cos_table - second * sin_table, first_half * sin_table + second * cos_table],
        axis=-1,
    )


def on_device(
    stream,
    lengths,
    q_weight,
    kv_down,
    latent_gain,
    kv_up,
    out_weight,
    moe_gain,
    routes,
    route_weight,
    expert_gate,
    expert_up,
    expert_down,
):
    tok_count = stream.shape[0]
    head_count = kv_up.shape[0]
    first_row = lax.axis_index("seq") * tok_count
    token_index = first_row + jnp.arange(tok_count, dtype=jnp.int32)
    segment, position = place(token_index, lengths)
    cos_table, sin_table = angles(position)
    kv_proj = jnp.dot(stream, kv_down, preferred_element_type=jnp.float32)
    compressed = kv_proj[:, :LATENT]
    factor = lax.rsqrt(jnp.mean(compressed * compressed, axis=1, keepdims=True) + 1e-06)
    latent = jnp.concatenate(
        [
            compressed * factor * latent_gain[None, :],
            rotate(kv_proj[:, LATENT:], cos_table, sin_table),
        ],
        axis=1,
    ).astype(jnp.bfloat16)
    q_proj = jnp.dot(stream, q_weight, preferred_element_type=jnp.float32).astype(jnp.bfloat16)
    q_proj = q_proj.reshape(tok_count, head_count, NOPE + ROPE)
    absorbed = jnp.einsum(
        "thj,hcj->thc", q_proj[:, :, :NOPE], kv_up[:, :, :NOPE], preferred_element_type=jnp.float32
    )
    rotated = rotate(
        q_proj[:, :, NOPE:].astype(jnp.float32), cos_table[:, None, :], sin_table[:, None, :]
    )
    softmax_scale = (NOPE + ROPE) ** (-0.5)
    queries = (jnp.concatenate([absorbed, rotated], axis=2) * softmax_scale).astype(jnp.bfloat16)
    queries = queries.reshape(tok_count * head_count, LATENT + ROPE)
    row_segment = jnp.repeat(segment, head_count)
    row_index = jnp.repeat(token_index, head_count)
    row_total = tok_count * head_count
    shard_rows = lax.all_gather(latent, "seq", axis=0, tiled=True)
    key_count = shard_rows.shape[0]
    key_index = jnp.arange(key_count, dtype=jnp.int32)
    key_segment, unused = place(key_index, lengths)
    allowed = (row_segment[:, None] == key_segment[None, :]) & (
        key_index[None, :] <= row_index[:, None]
    )
    running_max = jnp.full((row_total,), -1e30, jnp.float32)
    scores = jnp.einsum("ra,ka->rk", queries, shard_rows, preferred_element_type=jnp.float32)
    block_peak = jnp.max(jnp.where(allowed, scores, -jnp.inf), axis=1)
    new_peak = jnp.maximum(running_max, block_peak)
    weights = jnp.where(allowed, jnp.exp(scores - new_peak[:, None]), 0.0)
    running_sum = jnp.sum(weights, axis=1)
    context_sum = jnp.dot(
        weights.astype(jnp.bfloat16), shard_rows[:, :LATENT], preferred_element_type=jnp.float32
    )
    running_max, running_sum, context_sum = (new_peak, running_sum, context_sum)
    context = (context_sum / running_sum[:, None]).reshape(tok_count, head_count, LATENT)
    heads_out = jnp.einsum(
        "thc,hcv->thv",
        context,
        kv_up[:, :, NOPE:].astype(jnp.float32),
        precision=lax.Precision.HIGHEST,
    )
    heads_out = heads_out.astype(jnp.bfloat16).reshape(tok_count, head_count * VDIM)
    partial_attention = jnp.dot(heads_out, out_weight, preferred_element_type=jnp.float32)
    tp_count = lax.axis_size("tp")
    col_width = D // tp_count
    col_start = lax.axis_index("tp") * col_width
    attention_part = lax.psum_scatter(
        partial_attention.astype(jnp.bfloat16), "tp", scatter_dimension=1, tiled=True
    ).astype(jnp.float32)
    stream_part = lax.dynamic_slice_in_dim(stream, col_start, col_width, 1)
    hidden = stream_part.astype(jnp.float32) + attention_part
    normed = hidden.astype(jnp.bfloat16)
    experts = lax.axis_size("seq")
    top_k = routes.shape[1]
    capacity = min(tok_count, max(2, 2 * tok_count * top_k // experts))
    flat_routes = routes.reshape(-1)
    onehot = (flat_routes[:, None] == jnp.arange(experts, dtype=jnp.int32)[None, :]).astype(
        jnp.int32
    )
    slot_rank = jnp.sum((jnp.cumsum(onehot, axis=0) - onehot) * onehot, axis=1)
    slot_index = flat_routes * capacity + slot_rank
    slot_table = (
        slot_index[:, None] == jnp.arange(experts * capacity, dtype=jnp.int32)[None, :]
    ).astype(jnp.bfloat16)
    placing = jnp.sum(slot_table.reshape(tok_count, top_k, experts * capacity), axis=1)
    outgoing = jnp.einsum("ts,td->sd", placing, normed, preferred_element_type=jnp.float32).astype(
        jnp.bfloat16
    )
    outgoing = outgoing.reshape(experts, capacity, col_width)
    chunk_count = 2
    chunk_slots = capacity // chunk_count
    returned_chunks = []
    for chunk in range(chunk_count):
        sending = outgoing[:, chunk * chunk_slots : (chunk + 1) * chunk_slots]
        received = lax.all_to_all(sending, "seq", split_axis=0, concat_axis=0, tiled=True)
        sources, slot_count, _ = received.shape
        flat_part = received.reshape(sources * slot_count, col_width)
        if chunk == 0:
            flat_rows = lax.all_gather(flat_part, "tp", axis=1, tiled=True)
        else:
            repeated = jnp.broadcast_to(flat_part[None], (tp_count,) + flat_part.shape)
            pieces = lax.all_to_all(repeated, "tp", split_axis=0, concat_axis=0, tiled=True)
            flat_rows = pieces.transpose(1, 0, 2).reshape(sources * slot_count, D)
        flat_rows = flat_rows.astype(jnp.float32)
        flat_rows = (
            flat_rows
            * lax.rsqrt(jnp.mean(flat_rows * flat_rows, axis=1, keepdims=True) + 1e-06)
            * moe_gain[None, :]
        ).astype(jnp.bfloat16)
        gate_act = jnp.dot(flat_rows, expert_gate[0], preferred_element_type=jnp.float32)
        up_act = jnp.dot(flat_rows, expert_up[0], preferred_element_type=jnp.float32)
        hidden_units = (jax.nn.silu(gate_act) * up_act).astype(jnp.bfloat16)
        expert_out = jnp.dot(
            hidden_units, expert_down[0], preferred_element_type=jnp.float32
        ).astype(jnp.bfloat16)
        expert_sum = lax.psum_scatter(expert_out, "tp", scatter_dimension=1, tiled=True)
        expert_sum = expert_sum.reshape(sources, slot_count, col_width)
        returned_chunks.append(
            lax.all_to_all(expert_sum, "seq", split_axis=0, concat_axis=0, tiled=True)
        )
    returned = jnp.concatenate(returned_chunks, axis=1)
    gathered = returned.reshape(experts * capacity, col_width)[slot_index].reshape(
        tok_count, top_k, col_width
    )
    moe = jnp.zeros((tok_count, col_width), jnp.float32)
    for route_slot in range(top_k):
        moe = moe + route_weight[:, route_slot][:, None] * gathered[:, route_slot].astype(
            jnp.float32
        )
    layer_part = (hidden + moe).astype(jnp.bfloat16)
    layer_out = lax.all_gather(layer_part, "tp", axis=1, tiled=True)
    return (layer_out, latent)


def solution(mesh):
    return jax.shard_map(
        on_device,
        mesh=mesh,
        in_specs=(
            P("seq", None),
            P(),
            P(None, "tp"),
            P(),
            P(),
            P("tp", None, None),
            P("tp", None),
            P(),
            P("seq", None),
            P("seq", None),
            P("seq", None, "tp"),
            P("seq", None, "tp"),
            P("seq", "tp", None),
        ),
        out_specs=(P("seq", None), P("seq", None)),
        check_vma=False,
    )
```

```python
import jax
import jax.numpy as jnp
from jax import lax
from jax.sharding import PartitionSpec as P

D = 2048
NOPE = 128
ROPE = 64
LATENT = 512
VDIM = 128


THETA = 50000.0


def place(token_index, lengths):
    prompt_ends = jnp.cumsum(lengths)
    before = (prompt_ends[None, :] <= token_index[:, None]).astype(jnp.int32)
    segment = jnp.sum(before, axis=1)
    prompt_start = jnp.sum(before * lengths[None, :], axis=1)
    return (segment, token_index - prompt_start)


def angles(position):
    half_rope = ROPE // 2
    frequency = THETA ** (-2.0 * jnp.arange(half_rope, dtype=jnp.float32) / ROPE)
    angle_table = position.astype(jnp.float32)[:, None] * frequency[None, :]
    return (jnp.cos(angle_table), jnp.sin(angle_table))


def rotate(values, cos_table, sin_table):
    half_rope = ROPE // 2
    first_half = values[..., :half_rope]
    second = values[..., half_rope:]
    return jnp.concatenate(
        [first_half * cos_table - second * sin_table, first_half * sin_table + second * cos_table],
        axis=-1,
    )


def on_device(
    stream,
    lengths,
    q_weight,
    kv_down,
    latent_gain,
    kv_up,
    out_weight,
    moe_gain,
    routes,
    route_weight,
    expert_gate,
    expert_up,
    expert_down,
):
    tok_count = stream.shape[0]
    head_count = kv_up.shape[0]
    first_row = lax.axis_index("seq") * tok_count
    token_index = first_row + jnp.arange(tok_count, dtype=jnp.int32)
    segment, position = place(token_index, lengths)
    cos_table, sin_table = angles(position)
    kv_proj = jnp.dot(stream, kv_down, preferred_element_type=jnp.float32)
    compressed = kv_proj[:, :LATENT]
    factor = lax.rsqrt(jnp.mean(compressed * compressed, axis=1, keepdims=True) + 1e-06)
    latent = jnp.concatenate(
        [
            compressed * factor * latent_gain[None, :],
            rotate(kv_proj[:, LATENT:], cos_table, sin_table),
        ],
        axis=1,
    ).astype(jnp.bfloat16)
    q_proj = jnp.dot(stream, q_weight, preferred_element_type=jnp.float32).astype(jnp.bfloat16)
    q_proj = q_proj.reshape(tok_count, head_count, NOPE + ROPE)
    absorbed = jnp.einsum(
        "thj,hcj->thc", q_proj[:, :, :NOPE], kv_up[:, :, :NOPE], preferred_element_type=jnp.float32
    )
    rotated = rotate(
        q_proj[:, :, NOPE:].astype(jnp.float32), cos_table[:, None, :], sin_table[:, None, :]
    )
    softmax_scale = (NOPE + ROPE) ** (-0.5)
    queries = (jnp.concatenate([absorbed, rotated], axis=2) * softmax_scale).astype(jnp.bfloat16)
    queries = queries.reshape(tok_count * head_count, LATENT + ROPE)
    row_segment = jnp.repeat(segment, head_count)
    row_index = jnp.repeat(token_index, head_count)
    row_total = tok_count * head_count
    shard_rows = lax.all_gather(latent, "seq", axis=0, tiled=True)
    key_count = shard_rows.shape[0]
    key_index = jnp.arange(key_count, dtype=jnp.int32)
    key_segment, unused = place(key_index, lengths)
    allowed = (row_segment[:, None] == key_segment[None, :]) & (
        key_index[None, :] <= row_index[:, None]
    )
    running_max = jnp.full((row_total,), -1e30, jnp.float32)
    scores = jnp.einsum("ra,ka->rk", queries, shard_rows, preferred_element_type=jnp.float32)
    block_peak = jnp.max(jnp.where(allowed, scores, -jnp.inf), axis=1)
    new_peak = jnp.maximum(running_max, block_peak)
    weights = jnp.where(allowed, jnp.exp(scores - new_peak[:, None]), 0.0)
    running_sum = jnp.sum(weights, axis=1)
    context_sum = jnp.dot(
        weights.astype(jnp.bfloat16), shard_rows[:, :LATENT], preferred_element_type=jnp.float32
    )
    running_max, running_sum, context_sum = (new_peak, running_sum, context_sum)
    context = (context_sum / running_sum[:, None]).reshape(tok_count, head_count, LATENT)
    heads_out = jnp.einsum(
        "thc,hcv->thv",
        context,
        kv_up[:, :, NOPE:].astype(jnp.float32),
        precision=lax.Precision.HIGHEST,
    )
    heads_out = heads_out.astype(jnp.bfloat16).reshape(tok_count, head_count * VDIM)
    partial_attention = jnp.dot(heads_out, out_weight, preferred_element_type=jnp.float32)
    tp_count = lax.axis_size("tp")
    col_width = D // tp_count
    col_start = lax.axis_index("tp") * col_width
    attention_part = lax.psum_scatter(
        partial_attention.astype(jnp.bfloat16), "tp", scatter_dimension=1, tiled=True
    ).astype(jnp.float32)
    stream_part = lax.dynamic_slice_in_dim(stream, col_start, col_width, 1)
    hidden = stream_part.astype(jnp.float32) + attention_part
    normed = hidden.astype(jnp.bfloat16)
    experts = lax.axis_size("seq")
    top_k = routes.shape[1]
    capacity = min(tok_count, max(2, 2 * tok_count * top_k // experts))
    flat_routes = routes.reshape(-1)
    onehot = (flat_routes[:, None] == jnp.arange(experts, dtype=jnp.int32)[None, :]).astype(
        jnp.int32
    )
    slot_rank = jnp.sum((jnp.cumsum(onehot, axis=0) - onehot) * onehot, axis=1)
    slot_index = flat_routes * capacity + slot_rank
    slot_table = (
        slot_index[:, None] == jnp.arange(experts * capacity, dtype=jnp.int32)[None, :]
    ).astype(jnp.bfloat16)
    placing = jnp.sum(slot_table.reshape(tok_count, top_k, experts * capacity), axis=1)
    outgoing = jnp.einsum("ts,td->sd", placing, normed, preferred_element_type=jnp.float32).astype(
        jnp.bfloat16
    )
    outgoing = outgoing.reshape(experts, capacity, col_width)
    chunk_count = 2
    chunk_slots = capacity // chunk_count
    moe = jnp.zeros((tok_count, col_width), jnp.float32)
    for chunk in range(chunk_count):
        sending = outgoing[:, chunk * chunk_slots : (chunk + 1) * chunk_slots]
        received = lax.all_to_all(sending, "seq", split_axis=0, concat_axis=0, tiled=True)
        sources, slot_count, _ = received.shape
        flat_part = received.reshape(sources * slot_count, col_width)
        flat_rows = lax.all_gather(flat_part, "tp", axis=1, tiled=True).astype(jnp.float32)
        flat_rows = (
            flat_rows
            * lax.rsqrt(jnp.mean(flat_rows * flat_rows, axis=1, keepdims=True) + 1e-06)
            * moe_gain[None, :]
        ).astype(jnp.bfloat16)
        gate_act = jnp.dot(flat_rows, expert_gate[0], preferred_element_type=jnp.float32)
        up_act = jnp.dot(flat_rows, expert_up[0], preferred_element_type=jnp.float32)
        hidden_units = (jax.nn.silu(gate_act) * up_act).astype(jnp.bfloat16)
        expert_out = jnp.dot(
            hidden_units, expert_down[0], preferred_element_type=jnp.float32
        ).astype(jnp.bfloat16)
        expert_sum = lax.psum_scatter(expert_out, "tp", scatter_dimension=1, tiled=True)
        expert_sum = expert_sum.reshape(sources, slot_count, col_width)
        returned = lax.all_to_all(expert_sum, "seq", split_axis=0, concat_axis=0, tiled=True)
        in_chunk = (slot_rank // chunk_slots == chunk).reshape(tok_count, top_k)
        chunk_index = flat_routes * chunk_slots + slot_rank - chunk * chunk_slots
        chunk_index = jnp.where(in_chunk.reshape(-1), chunk_index, 0)
        gathered = returned.reshape(experts * chunk_slots, col_width)[chunk_index].reshape(
            tok_count, top_k, col_width
        )
        chunk_weight = jnp.where(in_chunk, route_weight, 0.0)
        for route_slot in range(top_k):
            moe = moe + chunk_weight[:, route_slot][:, None] * gathered[:, route_slot].astype(
                jnp.float32
            )
    layer_part = (hidden + moe).astype(jnp.bfloat16)
    layer_out = lax.all_gather(layer_part, "tp", axis=1, tiled=True)
    return (layer_out, latent)


def solution(mesh):
    return jax.shard_map(
        on_device,
        mesh=mesh,
        in_specs=(
            P("seq", None),
            P(),
            P(None, "tp"),
            P(),
            P(),
            P("tp", None, None),
            P("tp", None),
            P(),
            P("seq", None),
            P("seq", None),
            P("seq", None, "tp"),
            P("seq", None, "tp"),
            P("seq", "tp", None),
        ),
        out_specs=(P("seq", None), P("seq", None)),
        check_vma=False,
    )
```

```python
import jax
import jax.numpy as jnp
from jax import lax
from jax.sharding import PartitionSpec as P

D = 2048
NOPE = 128
ROPE = 64
LATENT = 512
VDIM = 128


THETA = 50000.0


def place(token_index, lengths):
    prompt_ends = jnp.cumsum(lengths)
    before = (prompt_ends[None, :] <= token_index[:, None]).astype(jnp.int32)
    segment = jnp.sum(before, axis=1)
    prompt_start = jnp.sum(before * lengths[None, :], axis=1)
    return (segment, token_index - prompt_start)


def angles(position):
    half_rope = ROPE // 2
    frequency = THETA ** (-2.0 * jnp.arange(half_rope, dtype=jnp.float32) / ROPE)
    angle_table = position.astype(jnp.float32)[:, None] * frequency[None, :]
    return (jnp.cos(angle_table), jnp.sin(angle_table))


def rotate(values, cos_table, sin_table):
    half_rope = ROPE // 2
    first_half = values[..., :half_rope]
    second = values[..., half_rope:]
    return jnp.concatenate(
        [first_half * cos_table - second * sin_table, first_half * sin_table + second * cos_table],
        axis=-1,
    )


def on_device(
    stream,
    lengths,
    q_weight,
    kv_down,
    latent_gain,
    kv_up,
    out_weight,
    moe_gain,
    routes,
    route_weight,
    expert_gate,
    expert_up,
    expert_down,
):
    tok_count = stream.shape[0]
    head_count = kv_up.shape[0]
    first_row = lax.axis_index("seq") * tok_count
    token_index = first_row + jnp.arange(tok_count, dtype=jnp.int32)
    segment, position = place(token_index, lengths)
    cos_table, sin_table = angles(position)
    kv_proj = jnp.dot(stream, kv_down, preferred_element_type=jnp.float32)
    compressed = kv_proj[:, :LATENT]
    factor = lax.rsqrt(jnp.mean(compressed * compressed, axis=1, keepdims=True) + 1e-06)
    latent = jnp.concatenate(
        [
            compressed * factor * latent_gain[None, :],
            rotate(kv_proj[:, LATENT:], cos_table, sin_table),
        ],
        axis=1,
    ).astype(jnp.bfloat16)
    q_proj = jnp.dot(stream, q_weight, preferred_element_type=jnp.float32).astype(jnp.bfloat16)
    q_proj = q_proj.reshape(tok_count, head_count, NOPE + ROPE)
    absorbed = jnp.einsum(
        "thj,hcj->thc", q_proj[:, :, :NOPE], kv_up[:, :, :NOPE], preferred_element_type=jnp.float32
    )
    rotated = rotate(
        q_proj[:, :, NOPE:].astype(jnp.float32), cos_table[:, None, :], sin_table[:, None, :]
    )
    softmax_scale = (NOPE + ROPE) ** (-0.5)
    queries = (jnp.concatenate([absorbed, rotated], axis=2) * softmax_scale).astype(jnp.bfloat16)
    queries = queries.reshape(tok_count * head_count, LATENT + ROPE)
    row_segment = jnp.repeat(segment, head_count)
    row_index = jnp.repeat(token_index, head_count)
    row_total = tok_count * head_count
    shard_rows = lax.all_gather(latent, "seq", axis=0, tiled=True)
    key_count = shard_rows.shape[0]
    key_index = jnp.arange(key_count, dtype=jnp.int32)
    key_segment, unused = place(key_index, lengths)
    allowed = (row_segment[:, None] == key_segment[None, :]) & (
        key_index[None, :] <= row_index[:, None]
    )
    running_max = jnp.full((row_total,), -1e30, jnp.float32)
    scores = jnp.einsum("ra,ka->rk", queries, shard_rows, preferred_element_type=jnp.float32)
    block_peak = jnp.max(jnp.where(allowed, scores, -jnp.inf), axis=1)
    new_peak = jnp.maximum(running_max, block_peak)
    weights = jnp.where(allowed, jnp.exp(scores - new_peak[:, None]), 0.0)
    running_sum = jnp.sum(weights, axis=1)
    context_sum = jnp.dot(
        weights.astype(jnp.bfloat16), shard_rows[:, :LATENT], preferred_element_type=jnp.float32
    )
    running_max, running_sum, context_sum = (new_peak, running_sum, context_sum)
    context = (context_sum / running_sum[:, None]).reshape(tok_count, head_count, LATENT)
    heads_out = jnp.einsum(
        "thc,hcv->thv",
        context,
        kv_up[:, :, NOPE:].astype(jnp.float32),
        precision=lax.Precision.HIGHEST,
    )
    heads_out = heads_out.astype(jnp.bfloat16).reshape(tok_count, head_count * VDIM)
    partial_attention = jnp.dot(heads_out, out_weight, preferred_element_type=jnp.float32)
    tp_count = lax.axis_size("tp")
    col_width = D // tp_count
    col_start = lax.axis_index("tp") * col_width
    attention_pieces = partial_attention.astype(jnp.bfloat16).reshape(tok_count, tp_count, col_width)
    attention_pieces = lax.all_to_all(
        attention_pieces.transpose(1, 0, 2), "tp", split_axis=0, concat_axis=0, tiled=True
    )
    attention_part = jnp.sum(attention_pieces.astype(jnp.float32), axis=0)
    stream_part = lax.dynamic_slice_in_dim(stream, col_start, col_width, 1)
    hidden = stream_part.astype(jnp.float32) + attention_part
    normed = hidden.astype(jnp.bfloat16)
    experts = lax.axis_size("seq")
    top_k = routes.shape[1]
    capacity = min(tok_count, max(2, 2 * tok_count * top_k // experts))
    flat_routes = routes.reshape(-1)
    onehot = (flat_routes[:, None] == jnp.arange(experts, dtype=jnp.int32)[None, :]).astype(
        jnp.int32
    )
    slot_rank = jnp.sum((jnp.cumsum(onehot, axis=0) - onehot) * onehot, axis=1)
    slot_index = flat_routes * capacity + slot_rank
    slot_table = (
        slot_index[:, None] == jnp.arange(experts * capacity, dtype=jnp.int32)[None, :]
    ).astype(jnp.bfloat16)
    placing = jnp.sum(slot_table.reshape(tok_count, top_k, experts * capacity), axis=1)
    outgoing = jnp.einsum("ts,td->sd", placing, normed, preferred_element_type=jnp.float32).astype(
        jnp.bfloat16
    )
    outgoing = outgoing.reshape(experts, capacity, col_width)
    chunk_count = 2
    chunk_slots = capacity // chunk_count
    returned_chunks = []
    for chunk in range(chunk_count):
        sending = outgoing[:, chunk * chunk_slots : (chunk + 1) * chunk_slots]
        received = lax.all_to_all(sending, "seq", split_axis=0, concat_axis=0, tiled=True)
        sources, slot_count, _ = received.shape
        flat_part = received.reshape(sources * slot_count, col_width)
        flat_rows = lax.all_gather(flat_part, "tp", axis=1, tiled=True).astype(jnp.float32)
        flat_rows = (
            flat_rows
            * lax.rsqrt(jnp.mean(flat_rows * flat_rows, axis=1, keepdims=True) + 1e-06)
            * moe_gain[None, :]
        ).astype(jnp.bfloat16)
        gate_act = jnp.dot(flat_rows, expert_gate[0], preferred_element_type=jnp.float32)
        up_act = jnp.dot(flat_rows, expert_up[0], preferred_element_type=jnp.float32)
        hidden_units = (jax.nn.silu(gate_act) * up_act).astype(jnp.bfloat16)
        expert_out = jnp.dot(
            hidden_units, expert_down[0], preferred_element_type=jnp.float32
        ).astype(jnp.bfloat16)
        expert_sum = lax.psum_scatter(expert_out, "tp", scatter_dimension=1, tiled=True)
        expert_sum = expert_sum.reshape(sources, slot_count, col_width)
        returned_chunks.append(
            lax.all_to_all(expert_sum, "seq", split_axis=0, concat_axis=0, tiled=True)
        )
    returned = jnp.concatenate(returned_chunks, axis=1)
    gathered = returned.reshape(experts * capacity, col_width)[slot_index].reshape(
        tok_count, top_k, col_width
    )
    moe = jnp.zeros((tok_count, col_width), jnp.float32)
    for route_slot in range(top_k):
        moe = moe + route_weight[:, route_slot][:, None] * gathered[:, route_slot].astype(
            jnp.float32
        )
    layer_part = (hidden + moe).astype(jnp.bfloat16)
    layer_out = lax.all_gather(layer_part, "tp", axis=1, tiled=True)
    return (layer_out, latent)


def solution(mesh):
    return jax.shard_map(
        on_device,
        mesh=mesh,
        in_specs=(
            P("seq", None),
            P(),
            P(None, "tp"),
            P(),
            P(),
            P("tp", None, None),
            P("tp", None),
            P(),
            P("seq", None),
            P("seq", None),
            P("seq", None, "tp"),
            P("seq", None, "tp"),
            P("seq", "tp", None),
        ),
        out_specs=(P("seq", None), P("seq", None)),
        check_vma=False,
    )
```

```python
import jax
import jax.numpy as jnp
from jax import lax
from jax.sharding import PartitionSpec as P

D = 2048
NOPE = 128
ROPE = 64
LATENT = 512
VDIM = 128


THETA = 50000.0


def place(token_index, lengths):
    prompt_ends = jnp.cumsum(lengths)
    before = (prompt_ends[None, :] <= token_index[:, None]).astype(jnp.int32)
    segment = jnp.sum(before, axis=1)
    prompt_start = jnp.sum(before * lengths[None, :], axis=1)
    return (segment, token_index - prompt_start)


def angles(position):
    half_rope = ROPE // 2
    frequency = THETA ** (-2.0 * jnp.arange(half_rope, dtype=jnp.float32) / ROPE)
    angle_table = position.astype(jnp.float32)[:, None] * frequency[None, :]
    return (jnp.cos(angle_table), jnp.sin(angle_table))


def rotate(values, cos_table, sin_table):
    half_rope = ROPE // 2
    first_half = values[..., :half_rope]
    second = values[..., half_rope:]
    return jnp.concatenate(
        [first_half * cos_table - second * sin_table, first_half * sin_table + second * cos_table],
        axis=-1,
    )


def on_device(
    stream,
    lengths,
    q_weight,
    kv_down,
    latent_gain,
    kv_up,
    out_weight,
    moe_gain,
    routes,
    route_weight,
    expert_gate,
    expert_up,
    expert_down,
):
    tok_count = stream.shape[0]
    head_count = kv_up.shape[0]
    first_row = lax.axis_index("seq") * tok_count
    token_index = first_row + jnp.arange(tok_count, dtype=jnp.int32)
    segment, position = place(token_index, lengths)
    cos_table, sin_table = angles(position)
    kv_proj = jnp.dot(stream, kv_down, preferred_element_type=jnp.float32)
    compressed = kv_proj[:, :LATENT]
    factor = lax.rsqrt(jnp.mean(compressed * compressed, axis=1, keepdims=True) + 1e-06)
    latent = jnp.concatenate(
        [
            compressed * factor * latent_gain[None, :],
            rotate(kv_proj[:, LATENT:], cos_table, sin_table),
        ],
        axis=1,
    ).astype(jnp.bfloat16)
    q_proj = jnp.dot(stream, q_weight, preferred_element_type=jnp.float32).astype(jnp.bfloat16)
    q_proj = q_proj.reshape(tok_count, head_count, NOPE + ROPE)
    absorbed = jnp.einsum(
        "thj,hcj->thc", q_proj[:, :, :NOPE], kv_up[:, :, :NOPE], preferred_element_type=jnp.float32
    )
    rotated = rotate(
        q_proj[:, :, NOPE:].astype(jnp.float32), cos_table[:, None, :], sin_table[:, None, :]
    )
    softmax_scale = (NOPE + ROPE) ** (-0.5)
    queries = (jnp.concatenate([absorbed, rotated], axis=2) * softmax_scale).astype(jnp.bfloat16)
    queries = queries.reshape(tok_count * head_count, LATENT + ROPE)
    row_segment = jnp.repeat(segment, head_count)
    row_index = jnp.repeat(token_index, head_count)
    row_total = tok_count * head_count
    shard_rows = lax.all_gather(latent, "seq", axis=0, tiled=True)
    key_count = shard_rows.shape[0]
    key_index = jnp.arange(key_count, dtype=jnp.int32)
    key_segment, unused = place(key_index, lengths)
    allowed = (row_segment[:, None] == key_segment[None, :]) & (
        key_index[None, :] <= row_index[:, None]
    )
    running_max = jnp.full((row_total,), -1e30, jnp.float32)
    scores = jnp.einsum("ra,ka->rk", queries, shard_rows, preferred_element_type=jnp.float32)
    block_peak = jnp.max(jnp.where(allowed, scores, -jnp.inf), axis=1)
    new_peak = jnp.maximum(running_max, block_peak)
    weights = jnp.where(allowed, jnp.exp(scores - new_peak[:, None]), 0.0)
    running_sum = jnp.sum(weights, axis=1)
    context_sum = jnp.dot(
        weights.astype(jnp.bfloat16), shard_rows[:, :LATENT], preferred_element_type=jnp.float32
    )
    running_max, running_sum, context_sum = (new_peak, running_sum, context_sum)
    context = (context_sum / running_sum[:, None]).reshape(tok_count, head_count, LATENT)
    heads_out = jnp.einsum(
        "thc,hcv->thv",
        context,
        kv_up[:, :, NOPE:].astype(jnp.float32),
        precision=lax.Precision.HIGHEST,
    )
    heads_out = heads_out.astype(jnp.bfloat16).reshape(tok_count, head_count * VDIM)
    partial_attention = jnp.dot(heads_out, out_weight, preferred_element_type=jnp.float32)
    tp_count = lax.axis_size("tp")
    col_width = D // tp_count
    col_start = lax.axis_index("tp") * col_width
    attention_pieces = partial_attention.astype(jnp.bfloat16).reshape(tok_count, tp_count, col_width)
    attention_pieces = lax.all_to_all(
        attention_pieces.transpose(1, 0, 2), "tp", split_axis=0, concat_axis=0, tiled=True
    )
    attention_part = jnp.sum(attention_pieces.astype(jnp.float32), axis=0)
    stream_part = lax.dynamic_slice_in_dim(stream, col_start, col_width, 1)
    hidden = stream_part.astype(jnp.float32) + attention_part
    normed = hidden.astype(jnp.bfloat16)
    experts = lax.axis_size("seq")
    top_k = routes.shape[1]
    capacity = min(tok_count, max(2, 2 * tok_count * top_k // experts))
    flat_routes = routes.reshape(-1)
    onehot = (flat_routes[:, None] == jnp.arange(experts, dtype=jnp.int32)[None, :]).astype(
        jnp.int32
    )
    slot_rank = jnp.sum((jnp.cumsum(onehot, axis=0) - onehot) * onehot, axis=1)
    slot_index = flat_routes * capacity + slot_rank
    slot_table = (
        slot_index[:, None] == jnp.arange(experts * capacity, dtype=jnp.int32)[None, :]
    ).astype(jnp.bfloat16)
    placing = jnp.sum(slot_table.reshape(tok_count, top_k, experts * capacity), axis=1)
    outgoing = jnp.einsum("ts,td->sd", placing, normed, preferred_element_type=jnp.float32).astype(
        jnp.bfloat16
    )
    outgoing = outgoing.reshape(experts, capacity, col_width)
    chunk_count = 2
    chunk_slots = capacity // chunk_count
    returned_chunks = []
    for chunk in range(chunk_count):
        sending = outgoing[:, chunk * chunk_slots : (chunk + 1) * chunk_slots]
        received = lax.all_to_all(sending, "seq", split_axis=0, concat_axis=0, tiled=True)
        sources, slot_count, _ = received.shape
        flat_part = received.reshape(sources * slot_count, col_width)
        flat_rows = lax.all_gather(flat_part, "tp", axis=1, tiled=True).astype(jnp.float32)
        flat_rows = (
            flat_rows
            * lax.rsqrt(jnp.mean(flat_rows * flat_rows, axis=1, keepdims=True) + 1e-06)
            * moe_gain[None, :]
        ).astype(jnp.bfloat16)
        gate_act = jnp.dot(flat_rows, expert_gate[0], preferred_element_type=jnp.float32)
        up_act = jnp.dot(flat_rows, expert_up[0], preferred_element_type=jnp.float32)
        hidden_units = (jax.nn.silu(gate_act) * up_act).astype(jnp.bfloat16)
        expert_out = jnp.dot(
            hidden_units, expert_down[0], preferred_element_type=jnp.float32
        ).astype(jnp.bfloat16)
        expert_sum = lax.psum_scatter(expert_out, "tp", scatter_dimension=1, tiled=True)
        expert_sum = expert_sum.reshape(sources, slot_count, col_width)
        returned_chunks.append(
            lax.all_to_all(expert_sum, "seq", split_axis=0, concat_axis=0, tiled=True)
        )
    returned = jnp.concatenate(returned_chunks, axis=1)
    gathered = returned.reshape(experts * capacity, col_width)[slot_index].reshape(
        tok_count, top_k, col_width
    )
    moe = jnp.zeros((tok_count, col_width), jnp.float32)
    for route_slot in range(top_k):
        moe = moe + route_weight[:, route_slot][:, None] * gathered[:, route_slot].astype(
            jnp.float32
        )
    layer_part = (hidden + moe).astype(jnp.bfloat16)
    repeated_part = jnp.broadcast_to(layer_part[None], (tp_count,) + layer_part.shape)
    layer_pieces = lax.all_to_all(repeated_part, "tp", split_axis=0, concat_axis=0, tiled=True)
    layer_out = layer_pieces.transpose(1, 0, 2).reshape(tok_count, D)
    return (layer_out, latent)


def solution(mesh):
    return jax.shard_map(
        on_device,
        mesh=mesh,
        in_specs=(
            P("seq", None),
            P(),
            P(None, "tp"),
            P(),
            P(),
            P("tp", None, None),
            P("tp", None),
            P(),
            P("seq", None),
            P("seq", None),
            P("seq", None, "tp"),
            P("seq", None, "tp"),
            P("seq", "tp", None),
        ),
        out_specs=(P("seq", None), P("seq", None)),
        check_vma=False,
    )
```

```python
import jax
import jax.numpy as jnp
from jax import lax
from jax.sharding import PartitionSpec as P

D = 2048
NOPE = 128
ROPE = 64
LATENT = 512
VDIM = 128


THETA = 50000.0


def place(token_index, lengths):
    prompt_ends = jnp.cumsum(lengths)
    before = (prompt_ends[None, :] <= token_index[:, None]).astype(jnp.int32)
    segment = jnp.sum(before, axis=1)
    prompt_start = jnp.sum(before * lengths[None, :], axis=1)
    return (segment, token_index - prompt_start)


def angles(position):
    half_rope = ROPE // 2
    frequency = THETA ** (-2.0 * jnp.arange(half_rope, dtype=jnp.float32) / ROPE)
    angle_table = position.astype(jnp.float32)[:, None] * frequency[None, :]
    return (jnp.cos(angle_table), jnp.sin(angle_table))


def rotate(values, cos_table, sin_table):
    half_rope = ROPE // 2
    first_half = values[..., :half_rope]
    second = values[..., half_rope:]
    return jnp.concatenate(
        [first_half * cos_table - second * sin_table, first_half * sin_table + second * cos_table],
        axis=-1,
    )


def on_device(
    stream,
    lengths,
    q_weight,
    kv_down,
    latent_gain,
    kv_up,
    out_weight,
    moe_gain,
    routes,
    route_weight,
    expert_gate,
    expert_up,
    expert_down,
):
    tok_count = stream.shape[0]
    head_count = kv_up.shape[0]
    first_row = lax.axis_index("seq") * tok_count
    token_index = first_row + jnp.arange(tok_count, dtype=jnp.int32)
    segment, position = place(token_index, lengths)
    cos_table, sin_table = angles(position)
    kv_proj = jnp.dot(stream, kv_down, preferred_element_type=jnp.float32)
    compressed = kv_proj[:, :LATENT]
    factor = lax.rsqrt(jnp.mean(compressed * compressed, axis=1, keepdims=True) + 1e-06)
    latent = jnp.concatenate(
        [
            compressed * factor * latent_gain[None, :],
            rotate(kv_proj[:, LATENT:], cos_table, sin_table),
        ],
        axis=1,
    ).astype(jnp.bfloat16)
    q_proj = jnp.dot(stream, q_weight, preferred_element_type=jnp.float32).astype(jnp.bfloat16)
    q_proj = q_proj.reshape(tok_count, head_count, NOPE + ROPE)
    absorbed = jnp.einsum(
        "thj,hcj->thc", q_proj[:, :, :NOPE], kv_up[:, :, :NOPE], preferred_element_type=jnp.float32
    )
    rotated = rotate(
        q_proj[:, :, NOPE:].astype(jnp.float32), cos_table[:, None, :], sin_table[:, None, :]
    )
    softmax_scale = (NOPE + ROPE) ** (-0.5)
    queries = (jnp.concatenate([absorbed, rotated], axis=2) * softmax_scale).astype(jnp.bfloat16)
    queries = queries.reshape(tok_count * head_count, LATENT + ROPE)
    row_segment = jnp.repeat(segment, head_count)
    row_index = jnp.repeat(token_index, head_count)
    row_total = tok_count * head_count
    shard_rows = lax.all_gather(latent, "seq", axis=0, tiled=True)
    key_count = shard_rows.shape[0]
    key_index = jnp.arange(key_count, dtype=jnp.int32)
    key_segment, unused = place(key_index, lengths)
    allowed = (row_segment[:, None] == key_segment[None, :]) & (
        key_index[None, :] <= row_index[:, None]
    )
    running_max = jnp.full((row_total,), -1e30, jnp.float32)
    scores = jnp.einsum("ra,ka->rk", queries, shard_rows, preferred_element_type=jnp.float32)
    block_peak = jnp.max(jnp.where(allowed, scores, -jnp.inf), axis=1)
    new_peak = jnp.maximum(running_max, block_peak)
    weights = jnp.where(allowed, jnp.exp(scores - new_peak[:, None]), 0.0)
    running_sum = jnp.sum(weights, axis=1)
    context_sum = jnp.dot(
        weights.astype(jnp.bfloat16), shard_rows[:, :LATENT], preferred_element_type=jnp.float32
    )
    running_max, running_sum, context_sum = (new_peak, running_sum, context_sum)
    context = (context_sum / running_sum[:, None]).reshape(tok_count, head_count, LATENT)
    heads_out = jnp.einsum(
        "thc,hcv->thv",
        context,
        kv_up[:, :, NOPE:].astype(jnp.float32),
        precision=lax.Precision.HIGHEST,
    )
    heads_out = heads_out.astype(jnp.bfloat16).reshape(tok_count, head_count * VDIM)
    partial_attention = jnp.dot(heads_out, out_weight, preferred_element_type=jnp.float32)
    tp_count = lax.axis_size("tp")
    col_width = D // tp_count
    col_start = lax.axis_index("tp") * col_width
    attention_pieces = partial_attention.astype(jnp.bfloat16).reshape(tok_count, tp_count, col_width)
    attention_pieces = lax.all_to_all(
        attention_pieces.transpose(1, 0, 2), "tp", split_axis=0, concat_axis=0, tiled=True
    )
    attention_part = jnp.sum(attention_pieces.astype(jnp.float32), axis=0)
    stream_part = lax.dynamic_slice_in_dim(stream, col_start, col_width, 1)
    hidden = stream_part.astype(jnp.float32) + attention_part
    normed = hidden.astype(jnp.bfloat16)
    experts = lax.axis_size("seq")
    top_k = routes.shape[1]
    capacity = min(tok_count, max(2, 2 * tok_count * top_k // experts))
    flat_routes = routes.reshape(-1)
    onehot = (flat_routes[:, None] == jnp.arange(experts, dtype=jnp.int32)[None, :]).astype(
        jnp.int32
    )
    slot_rank = jnp.sum((jnp.cumsum(onehot, axis=0) - onehot) * onehot, axis=1)
    slot_index = flat_routes * capacity + slot_rank
    slot_table = (
        slot_index[:, None] == jnp.arange(experts * capacity, dtype=jnp.int32)[None, :]
    ).astype(jnp.bfloat16)
    placing = jnp.sum(slot_table.reshape(tok_count, top_k, experts * capacity), axis=1)
    outgoing = jnp.einsum("ts,td->sd", placing, normed, preferred_element_type=jnp.float32).astype(
        jnp.bfloat16
    )
    outgoing = outgoing.reshape(experts, capacity, col_width)
    chunk_count = 2
    chunk_slots = capacity // chunk_count
    returned_chunks = []
    received_all = lax.all_to_all(outgoing, "seq", split_axis=0, concat_axis=0, tiled=True)
    for chunk in range(chunk_count):
        received = received_all[:, chunk * chunk_slots : (chunk + 1) * chunk_slots]
        sources, slot_count, _ = received.shape
        flat_part = received.reshape(sources * slot_count, col_width)
        flat_rows = lax.all_gather(flat_part, "tp", axis=1, tiled=True).astype(jnp.float32)
        flat_rows = (
            flat_rows
            * lax.rsqrt(jnp.mean(flat_rows * flat_rows, axis=1, keepdims=True) + 1e-06)
            * moe_gain[None, :]
        ).astype(jnp.bfloat16)
        gate_act = jnp.dot(flat_rows, expert_gate[0], preferred_element_type=jnp.float32)
        up_act = jnp.dot(flat_rows, expert_up[0], preferred_element_type=jnp.float32)
        hidden_units = (jax.nn.silu(gate_act) * up_act).astype(jnp.bfloat16)
        expert_out = jnp.dot(
            hidden_units, expert_down[0], preferred_element_type=jnp.float32
        ).astype(jnp.bfloat16)
        expert_sum = lax.psum_scatter(expert_out, "tp", scatter_dimension=1, tiled=True)
        expert_sum = expert_sum.reshape(sources, slot_count, col_width)
        returned_chunks.append(
            lax.all_to_all(expert_sum, "seq", split_axis=0, concat_axis=0, tiled=True)
        )
    returned = jnp.concatenate(returned_chunks, axis=1)
    gathered = returned.reshape(experts * capacity, col_width)[slot_index].reshape(
        tok_count, top_k, col_width
    )
    moe = jnp.zeros((tok_count, col_width), jnp.float32)
    for route_slot in range(top_k):
        moe = moe + route_weight[:, route_slot][:, None] * gathered[:, route_slot].astype(
            jnp.float32
        )
    layer_part = (hidden + moe).astype(jnp.bfloat16)
    repeated_part = jnp.broadcast_to(layer_part[None], (tp_count,) + layer_part.shape)
    layer_pieces = lax.all_to_all(repeated_part, "tp", split_axis=0, concat_axis=0, tiled=True)
    layer_out = layer_pieces.transpose(1, 0, 2).reshape(tok_count, D)
    return (layer_out, latent)


def solution(mesh):
    return jax.shard_map(
        on_device,
        mesh=mesh,
        in_specs=(
            P("seq", None),
            P(),
            P(None, "tp"),
            P(),
            P(),
            P("tp", None, None),
            P("tp", None),
            P(),
            P("seq", None),
            P("seq", None),
            P("seq", None, "tp"),
            P("seq", None, "tp"),
            P("seq", "tp", None),
        ),
        out_specs=(P("seq", None), P("seq", None)),
        check_vma=False,
    )
```
